32 devices in a mesh: seq: 8 (over z, y), chan: 4 (over x, core).
Axes of the slice: x: 2, y: 2, z: 4, core: 2. Of those that a mesh axis runs over, the one named last changes fastest.
Arguments:
- proj_in: bfloat16 [3, 1024, 4096], P(None, 'seq', 'chan'), may hold values from -6 to 6
- taps: float32 [3, 3, 4096], P(None, None, 'chan'), may hold values from -3 to 3
- long_filter: float32 [1024, 256], P('seq'), may hold values from -6 to 6
- out_grad: bfloat16 [1024, 4096], P('seq', 'chan'), may hold values from -0.1875 to 0.1875
Outputs:
- input_grad: bfloat16 [3, 1024, 4096], P(None, 'seq', 'chan')
- long_grad: float32 [1024, 256], P('seq', 'chan')
- tap_grad: float32 [3, 3, 4096], P(None, None, 'chan')
The draws below stay inside these ranges and needn't reach their ends.
All inputs are finite; a program needn't handle non-finite values.
Results may differ from the reference program's by a relative error of at most 0.001.
Values may be sent and summed in bfloat16 or wider, within the bound.
A program may use at most 64 MiB of HBM per device.

```python
import math
import jax
import jax.numpy as jnp
from jax import lax

D = 4096
G = 256
K = 3
TOKENS = 1024


def steps_of(own_key, extent, split, smallest, top_value):
    loudness = 1.0
    for position, blocks in split:
        draws = jax.random.uniform(jax.random.fold_in(jax.random.fold_in(own_key, 6), position), (blocks,), jnp.float32, smallest / len(split), top_value / len(split))
        loudness = loudness * jnp.repeat(jnp.exp(draws), extent[position] // blocks).reshape((-1,) + (1,) * (len(extent) - 1 - position))
    return loudness


def bell_draw(rng, extent, width, bound, cuts=(), held_as=jnp.bfloat16):
    entries = jax.random.normal(rng, extent, jnp.float32) * width
    if len(cuts) > 0:
        entries = steps_of(rng, extent, cuts, -0.22, 0.18) * entries
    return jnp.clip(entries, min=-bound, max=bound).astype(held_as)


def setup_inputs(seed: int = 0) -> dict:
    splits = jax.random.split(jax.random.key(seed), 5)
    proj_in = bell_draw(splits[0], (3, TOKENS, D), 1.0, 6.0, ((1, 8), (2, 4)))
    taps = bell_draw(splits[1], (3, K, D), 0.6, 3.0, ((2, 4),), jnp.float32)
    long_filter = bell_draw(splits[2], (TOKENS, G), 1.0, 6.0, ((0, 8),), jnp.float32)
    out_grad = bell_draw(splits[3], (TOKENS, D), TOKENS ** -0.5, 0.1875, ((0, 8), (1, 4)))
    return {"proj_in": proj_in, "taps": taps, "long_filter": long_filter, "out_grad": out_grad}


def delayed(values, lag_step):
    if lag_step == 0:
        return values
    padding = jnp.zeros((values.shape[0], lag_step, values.shape[2]), values.dtype)
    return jnp.concatenate([padding, values[:, :values.shape[1] - lag_step]], axis=1)

def advanced(values, lag_step):
    if lag_step == 0:
        return values
    padding = jnp.zeros((values.shape[0], lag_step, values.shape[2]), values.dtype)
    return jnp.concatenate([values[:, lag_step:], padding], axis=1)

def reference(proj_in, taps, long_filter, out_grad):
    inputs = proj_in.astype(jnp.float32)
    lagged = [delayed(inputs, lag_step) for lag_step in range(K)]
    featured = taps[:, 0, None, :] * lagged[0]
    for lag_step in range(1, K):
        featured = featured + taps[:, lag_step, None, :] * lagged[lag_step]
    query_rows, key_rows, value_rows = (featured[0], featured[1], featured[2])
    mixed_rows = key_rows * value_rows
    upstream = out_grad.astype(jnp.float32)
    conv_grad = upstream * query_rows
    length = 2 * TOKENS
    blocks = D // G
    filt_spec = jnp.fft.rfft(long_filter, n=length, axis=0)
    mixed_blocks = mixed_rows.reshape(TOKENS, blocks, G).transpose(1, 0, 2)
    grad_blocks = conv_grad.reshape(TOKENS, blocks, G).transpose(1, 0, 2)

    def one_block(pair):
        mixed_part, grad_part = pair
        mix_spec = jnp.fft.rfft(mixed_part, n=length, axis=0)
        grad_spec = jnp.fft.rfft(grad_part, n=length, axis=0)
        conv_part = jnp.fft.irfft(filt_spec * mix_spec, n=length, axis=0)[:TOKENS]
        back_part = jnp.fft.irfft(jnp.conj(filt_spec) * grad_spec, n=length, axis=0)[:TOKENS]
        corr_part = jnp.fft.irfft(grad_spec * jnp.conj(mix_spec), n=length, axis=0)[:TOKENS]
        return (conv_part, back_part, corr_part)
    conv_blocks, back_blocks, corr_blocks = lax.map(one_block, (mixed_blocks, grad_blocks))
    conv_out = conv_blocks.transpose(1, 0, 2).reshape(TOKENS, D)
    mixed_grad = back_blocks.transpose(1, 0, 2).reshape(TOKENS, D)
    long_grad = lax.optimization_barrier(jnp.sum(corr_blocks, axis=0))
    feature_grad = jnp.stack([upstream * conv_out, mixed_grad * value_rows, mixed_grad * key_rows], axis=0)
    input_grad = taps[:, 0, None, :] * feature_grad
    for lag_step in range(1, K):
        input_grad = input_grad + taps[:, lag_step, None, :] * advanced(feature_grad, lag_step)
    tap_grad = jnp.stack([lax.optimization_barrier(jnp.sum(feature_grad * lagged[lag_step], axis=1)) for lag_step in range(K)], axis=1)
    tap_grad = tap_grad / math.sqrt(TOKENS)
    return (input_grad.astype(jnp.bfloat16), long_grad, tap_grad)
```

```python
import functools
import math

import jax
import jax.numpy as jnp
import numpy as np
from jax import lax
from jax.experimental import pallas as pl
from jax.experimental.pallas import tpu as pltpu
from jax.sharding import PartitionSpec as P

MESH = pl.DeviceIdType.MESH
LANES = 128
TABLE_LIMIT = 1024
LEVELS = 250.0
RIM = 2


def shifted(x, axis, by):
    devices = lax.axis_size(axis)
    pairs = [(i, i + by) for i in range(devices) if 0 <= i + by < devices]
    return lax.ppermute(x, axis, pairs)


def angle_table(left_index, right_index, period):
    product = left_index[:, None] * right_index[None, :] % period
    phase = product.astype(jnp.float32) * (2.0 * math.pi / period)
    return (jnp.cos(phase), jnp.sin(phase))


def contract(pattern, factor_table, operand):
    return jnp.einsum(pattern, factor_table, operand, precision=lax.Precision.HIGHEST)


def steps_of(count):
    return jnp.arange(count, dtype=jnp.int32)


def whole_forward(signal, seq_width):
    tok_rows, stack_count, channels = signal.shape
    period = 2 * seq_width * tok_rows
    narrow = channels // seq_width
    arrived = lax.all_to_all(signal, "seq", split_axis=2, concat_axis=0, tiled=True)
    laid = arrived.reshape(seq_width, tok_rows, stack_count, narrow).transpose(2, 3, 0, 1)
    cos_step, sin_step = angle_table(steps_of(2 * seq_width), steps_of(seq_width), 2 * seq_width)
    real_part = contract("qm,ncmj->ncqj", cos_step, laid)
    imag_part = -contract("qm,ncmj->ncqj", sin_step, laid)
    cos_turn, sin_turn = angle_table(steps_of(2 * seq_width), steps_of(tok_rows), period)
    turned_re = real_part * cos_turn + imag_part * sin_turn
    turned_im = imag_part * cos_turn - real_part * sin_turn
    cos_row, sin_row = angle_table(steps_of(tok_rows), steps_of(tok_rows), tok_rows)
    spec_re = contract("rj,ncqj->ncqr", cos_row, turned_re) + contract(
        "rj,ncqj->ncqr", sin_row, turned_im
    )
    spec_im = contract("rj,ncqj->ncqr", cos_row, turned_im) - contract(
        "rj,ncqj->ncqr", sin_row, turned_re
    )
    return (spec_re, spec_im)


def whole_inverse(spec_re, spec_im, seq_width):
    stack_count, narrow, freq_count, tok_rows = spec_re.shape
    period = 2 * seq_width * tok_rows
    cos_row, sin_row = angle_table(steps_of(tok_rows), steps_of(tok_rows), tok_rows)
    back_re = contract("rj,ncqr->ncqj", cos_row, spec_re) - contract(
        "rj,ncqr->ncqj", sin_row, spec_im
    )
    back_im = contract("rj,ncqr->ncqj", sin_row, spec_re) + contract(
        "rj,ncqr->ncqj", cos_row, spec_im
    )
    cos_turn, sin_turn = angle_table(steps_of(freq_count), steps_of(tok_rows), period)
    turned_re = back_re * cos_turn - back_im * sin_turn
    turned_im = back_re * sin_turn + back_im * cos_turn
    cos_step, sin_step = angle_table(steps_of(seq_width), steps_of(freq_count), freq_count)
    signal = contract("mq,ncqj->ncmj", cos_step, turned_re) - contract(
        "mq,ncqj->ncmj", sin_step, turned_im
    )
    signal = (
        (signal / period).transpose(2, 3, 0, 1).reshape(seq_width * tok_rows, stack_count, narrow)
    )
    return lax.all_to_all(signal, "seq", split_axis=0, concat_axis=2, tiled=True)


def member(values, index, stack_axis):
    return lax.index_in_dim(values, index, stack_axis, keepdims=False)


def shards(proj_in, taps, long_filter, out_grad):
    stream_count, tok_rows, channels = proj_in.shape
    tap_count = taps.shape[1]
    groups = long_filter.shape[1]
    seq_width = lax.axis_size("seq")
    lower_rim = shifted(proj_in[:, tok_rows - (tap_count - 1) :, :], "seq", 1)
    extended = jnp.concatenate([lower_rim, proj_in], axis=1).astype(jnp.float32)
    lagged = [
        extended[:, tap_count - 1 - lag_step : tap_count - 1 - lag_step + tok_rows, :]
        for lag_step in range(tap_count)
    ]
    featured = taps[:, 0, None, :] * lagged[0]
    for lag_step in range(1, tap_count):
        featured = featured + taps[:, lag_step, None, :] * lagged[lag_step]
    query_rows, key_rows, value_rows = (featured[0], featured[1], featured[2])
    mixed_rows = key_rows * value_rows
    upstream = out_grad.astype(jnp.float32)
    conv_grad = upstream * query_rows
    tiled_filter = jnp.tile(long_filter, (1, channels // groups))
    signals = jnp.stack([mixed_rows, conv_grad, tiled_filter], axis=1)
    data_re, data_im = whole_forward(signals, seq_width)
    stack_axis = 0
    mix_re, mix_im = (member(data_re, 0, stack_axis), member(data_im, 0, stack_axis))
    grad_re, grad_im = (member(data_re, 1, stack_axis), member(data_im, 1, stack_axis))
    filt_re, filt_im = (member(data_re, 2, stack_axis), member(data_im, 2, stack_axis))
    conv_re = filt_re * mix_re - filt_im * mix_im
    conv_im = filt_re * mix_im + filt_im * mix_re
    back_re = filt_re * grad_re + filt_im * grad_im
    back_im = filt_re * grad_im - filt_im * grad_re
    corr_re = grad_re * mix_re + grad_im * mix_im
    corr_im = grad_im * mix_re - grad_re * mix_im
    prod_re = jnp.stack([conv_re, back_re, corr_re], axis=stack_axis)
    prod_im = jnp.stack([conv_im, back_im, corr_im], axis=stack_axis)
    outputs = whole_inverse(prod_re, prod_im, seq_width)
    conv_out, mixed_grad = (outputs[:, 0], outputs[:, 1])
    filt_grad = jnp.sum(outputs[:, 2].reshape(tok_rows, channels // groups, groups), axis=1)
    long_grad = lax.psum_scatter(filt_grad, "chan", scatter_dimension=1, tiled=True)
    feature_grad = jnp.stack(
        [upstream * conv_out, mixed_grad * value_rows, mixed_grad * key_rows], axis=0
    )
    upper_rim = shifted(feature_grad[:, : tap_count - 1, :], "seq", -1)
    trailing = jnp.concatenate([feature_grad, upper_rim], axis=1)
    input_grad = taps[:, 0, None, :] * feature_grad
    for lag_step in range(1, tap_count):
        input_grad = (
            input_grad + taps[:, lag_step, None, :] * trailing[:, lag_step : lag_step + tok_rows]
        )
    partial_taps = jnp.stack(
        [jnp.sum(feature_grad * lagged[lag_step], axis=1) for lag_step in range(tap_count)], axis=1
    )
    tap_grad = lax.psum(partial_taps, "seq") / math.sqrt(seq_width * tok_rows)
    return (input_grad.astype(jnp.bfloat16), long_grad, tap_grad)


def greet(axis_sizes):
    barrier = pltpu.get_barrier_semaphore()
    for axis, size in axis_sizes:
        me = lax.axis_index(axis)
        for j in range(1, size):
            pl.semaphore_signal(
                barrier, inc=1, device_id={axis: lax.rem(me + j, size)}, device_id_type=MESH
            )


def welcome(sizes):
    pl.semaphore_wait(pltpu.get_barrier_semaphore(), sum(size - 1 for size in sizes))


def swap_matrix(reps, width):
    side = reps * LANES
    row, col = np.arange(side)[:, None], np.arange(side)[None, :]
    outer, inner, rest = row // LANES, (row % LANES) // width, row % width
    return (inner * LANES + outer * width + rest == col).astype(jnp.bfloat16)


def lane_group(rows, width):
    return lax.broadcasted_iota(jnp.int32, (rows, LANES), 1) // width


def row_of(shape):
    return lax.broadcasted_iota(jnp.int32, shape, 0)


def turn(x, shift, axis):
    shift = shift % x.shape[axis]
    return x if shift == 0 else pltpu.roll(x, shift, axis)


def halves(x):
    high = x.astype(jnp.bfloat16)
    return high, (x - high.astype(jnp.float32)).astype(jnp.bfloat16)


def later(x):
    return jnp.where(row_of(x.shape) < 1, 0.0, pltpu.roll(x, 1, 0))


def sooner(x):
    rows = x.shape[0]
    return jnp.where(row_of(x.shape) >= rows - 1, 0.0, pltpu.roll(x, rows - 1, 0))


def group_sum(x, reps):
    step = LANES // reps
    if reps & (reps - 1):
        return sum((turn(x, r * step, 1) for r in range(1, reps)), x)
    while step < LANES:
        x = x + turn(x, step, 1)
        step *= 2
    return x


def encode(x):
    size = jnp.abs(x)
    first = jnp.where(row_of((8, LANES)) < RIM, 0.0, size[:8])
    top = jnp.max(jnp.concatenate([first, size[8:]], axis=0), axis=0, keepdims=True)
    scale = jnp.maximum(top * (1.0 + 2.0**-7), 1e-30).astype(jnp.bfloat16).astype(jnp.float32)
    level = jnp.exp2(size * (LEVELS / scale) - 0.5 * LEVELS)
    level = jnp.where(x < 0.0, -level, level)
    first = jnp.where(row_of((8, LANES)) < RIM, scale, level[:8])
    return jnp.concatenate([first, level[8:]], axis=0).astype(jnp.bfloat16)


def decode(code):
    scale = code[:1]
    size = (jnp.log(jnp.abs(code)) * (1.0 / (math.log(2.0) * LEVELS)) + 0.5) * scale
    return jnp.where(code < 0.0, -size, size)


def dot(left, right):
    return jnp.dot(left, right, preferred_element_type=jnp.float32)


def paired(high, low, both):
    wide = dot(high, both)
    return wide[:, :LANES] + (wide[:, LANES:] + dot(low, both[:, :LANES]))


def alternating(count):
    return jnp.where(row_of((count, LANES)) % 2 == 0, 1.0, -1.0)


def whole_kernel(
    n, m, reps, x_ref, og_ref, lf_ref, tp_ref, sw_ref, tb_hbm, out_ref, lo_ref, to_ref,
    tb, ex, es, er, exf, xs, xr, kf, vf, fs, fr, buf, both_e, both_o, fsp, gsp, pq_e, pq_o, half_out,
    codes, igr, back, backr, lgs, lgc, lsum, lgr, l2, ts, tr, tsum, tg, us, ug, lsem, sems, csems,
):
    me, mine = lax.axis_index("seq"), lax.axis_index("chan")
    width = LANES // reps
    streams, rows, _ = x_ref.shape
    tap_count = tp_ref.shape[1]
    tokens = n * rows
    half = tokens // 2
    near = n // 2
    part = rows // reps
    share = part // m
    tiles = n // reps
    f32, bf16 = jnp.float32, jnp.bfloat16
    fetched = pltpu.make_async_copy(tb_hbm, tb, lsem.at[0])
    fetched.start()
    grp = lane_group(part, width)
    greet([("seq", n), ("chan", m)])

    def remote(kind, slot, source, target, peer):
        copy = pltpu.make_async_remote_copy(
            src_ref=source, dst_ref=target, send_sem=sems.at[0, kind, slot],
            recv_sem=sems.at[1, kind, slot], device_id={"seq": peer}, device_id_type=MESH,
        )
        copy.start()
        return copy

    def ship(kind, source, target):
        return [
            remote(kind, j - 1, source(lax.rem(me + j, n)), target, lax.rem(me + j, n))
            for j in sorted(range(1, n), key=lambda j: abs(2 * j - n))
        ]

    def spread(kind, source, target):
        copies = []
        for j in range(1, m):
            peer = lax.rem(mine + j, m)
            copy = pltpu.make_async_remote_copy(
                src_ref=source(peer), dst_ref=target, send_sem=csems.at[0, kind, j - 1],
                recv_sem=csems.at[1, kind, j - 1], device_id={"chan": peer}, device_id_type=MESH,
            )
            copy.start()
            copies.append(copy)
        return copies

    def place(r, h):
        return slice((r * tiles + h) * LANES, (r * tiles + h + 1) * LANES)

    def feature(p, at):
        x = x_ref[p, :, at].astype(f32)
        total = tp_ref[p, 0:1, at] * x
        for lag in range(1, tap_count):
            total = total + tp_ref[p, lag : lag + 1, at] * pltpu.roll(x, lag, 0)
        return total

    def send_layout(pieces, place_at):
        moved = dot(jnp.concatenate(pieces, axis=1), sw_ref[...]).astype(bf16)
        for g in range(reps):
            place_at(g)[...] = moved[:, g * LANES : (g + 1) * LANES]

    for s in range(n):
        base = (s // reps) * LANES
        packed = jnp.zeros((part, LANES), f32)
        for q in range(reps):
            tile = lf_ref[q * part : (q + 1) * part, base : base + LANES]
            packed = jnp.where(grp == q, turn(tile, (q - s % reps) * width, 1), packed)
        fs[s] = packed.reshape(m, share, LANES)
    ex[...] = jnp.zeros_like(ex)
    for p in range(streams):
        ex[RIM * p : RIM * (p + 1), :] = x_ref[p, :16, :].astype(f32)[:RIM]
        ex[8 + RIM * p : 8 + RIM * (p + 1), :] = x_ref[p, rows - 16 :, :].astype(f32)[16 - RIM :]
    ex[RIM * streams : RIM * (streams + 1), :] = og_ref[:16, :].astype(f32)[:RIM]
    for h in range(tiles):
        send_layout(
            [ex[:, place(r, h)].astype(bf16) for r in range(reps)], lambda g: es.at[h * reps + g]
        )
        send_layout(
            [
                encode(og_ref[:, place(r, h)].astype(f32) * feature(0, place(r, h)))
                for r in range(reps)
            ],
            lambda g: xs.at[0, h * reps + g],
        )
    welcome([n, m])
    filter_sent = ship(0, lambda peer: fs.at[peer, mine], fr.at[mine, me])
    rims_sent = ship(1, lambda peer: es.at[peer], er.at[me])
    first = ship(2, lambda peer: xs.at[0, peer], xr.at[0, me])
    for h in range(tiles):
        pieces = []
        for r in range(reps):
            at = place(r, h)
            key, value = feature(1, at), feature(2, at)
            kf[:, at], vf[:, at] = key, value
            pieces.append(encode(key * value))
        send_layout(pieces, lambda g: xs.at[1, h * reps + g])
    second = ship(3, lambda peer: xs.at[1, peer], xr.at[1, me])
    fr[mine, me] = fs[me, mine]
    er[me] = es[me]
    xr[0, me] = xs[0, me]
    xr[1, me] = xs[1, me]

    taps = []
    home, slot = me // reps, lax.rem(me, reps)
    for p in range(streams):
        mixed_taps = jnp.zeros((tap_count, LANES), f32)
        for r in range(reps):
            at = pl.multiple_of((r * tiles + home) * LANES, LANES)
            tile = tp_ref[p, :, pl.ds(at, LANES)]
            shift = lax.rem((r + reps - slot) * width, LANES)
            mixed_taps = jnp.where(
                lane_group(tap_count, width) == r, pltpu.roll(tile, shift, 1), mixed_taps
            )
        taps.append([mixed_taps[i : i + 1] for i in range(tap_count)])

    def split():
        ends = []
        for part_of, both in ((0, both_e), (1, both_o)):
            values = buf[pl.ds(part_of, half, stride=2), :]
            both[:, :LANES], both[:, LANES:] = halves(values)
            ends.append(jnp.sum(alternating(half) * values, axis=0, keepdims=True))
        return ends

    chunk = min(256, half)

    def spectra(at):
        return [
            paired(tb[table, 0, at, :], tb[table, 1, at, :], both[...])
            for table, both in ((0, both_e), (1, both_e), (2, both_o), (3, both_o))
        ]

    def store_products(at, low, even_cos, even_sin, odd_cos, odd_sin):
        pq_e[at, :LANES], pq_e[at, LANES:] = halves(even_cos)
        pq_e[low, :LANES], pq_e[low, LANES:] = halves(even_sin)
        pq_o[at, :LANES], pq_o[at, LANES:] = halves(odd_cos)
        pq_o[low, :LANES], pq_o[low, LANES:] = halves(odd_sin)

    def inverse(at, end_e, end_o):
        even = paired(tb[0, 0, at, :], tb[0, 1, at, :], pq_e[:half])
        even = even + paired(tb[1, 0, at, :], tb[1, 1, at, :], pq_e[half:])
        odd = paired(tb[4, 0, at, :], tb[4, 1, at, :], pq_o[:half])
        odd = odd + paired(tb[5, 0, at, :], tb[5, 1, at, :], pq_o[half:])
        sign = alternating(even.shape[0])
        return even + sign * end_e, odd + sign * end_o

    def return_layout(kind, end_e, end_o):
        copies = []
        side = me // near
        for step in range(2):
            which = (1 - side) if step == 0 else side
            for c in range(half // 2 // chunk):
                at = pl.ds(pl.multiple_of(which * (half // 2) + c * chunk, chunk), chunk)
                even, odd = inverse(at, end_e, end_o)
                half_out[step, pl.ds(2 * c * chunk, chunk, stride=2), :] = even
                half_out[step, pl.ds(2 * c * chunk + 1, chunk, stride=2), :] = odd
            for i in range(near):
                codes[kind, step, i] = encode(half_out[step, i * rows : (i + 1) * rows, :])
            for i in range(step, near):
                inner = lax.rem(me + i, near)
                copies.append(
                    remote(
                        4 + 2 * kind, step * near + i - step, codes.at[kind, step, inner],
                        igr.at[kind, me], which * near + inner,
                    )
                )
        igr[kind, me] = codes[kind, 1, lax.rem(me, near)]
        rims = []
        for i in range(RIM):
            far_rows = half_out[0, pl.ds(i, near, stride=rows), :]
            near_rows = half_out[1, pl.ds(i, near, stride=rows), :]
            low = jnp.where(side == 0, near_rows, far_rows)
            high = jnp.where(side == 0, far_rows, near_rows)
            rims.append(jnp.concatenate([low, high], axis=0))
        return copies, rims

    def return_rims(kind, grads):
        if len(grads) == 1:
            back[kind, ...] = jnp.zeros_like(back[kind])
        for k, pair in enumerate(grads):
            for i in range(RIM):
                back[kind, pl.ds(RIM * k + i, n, stride=8), :] = pair[i]
                back[kind, pl.ds(RIM * (k + len(grads)) + i, n, stride=8), :] = sooner(pair[i])
        mine_at = pl.ds(pl.multiple_of(me * 8, 8), 8)
        backr[kind, mine_at, :] = back[kind, mine_at, :]
        return ship(
            5 + 2 * kind, lambda peer: back.at[kind, pl.ds(pl.multiple_of(peer * 8, 8), 8)],
            backr.at[kind, mine_at],
        )

    for copy in filter_sent:
        copy.wait()
    filter_passed = spread(0, lambda peer: fr.at[mine], fr.at[mine])
    for copy in rims_sent:
        copy.wait()
    exf[...] = er[...].reshape(n * 16, LANES).astype(f32)

    def rim(i):
        return exf[pl.ds(i, n, stride=16), :]

    def rim_feature(p):
        now, before = [rim(RIM * p), rim(RIM * p + 1)], [rim(8 + RIM * p + 1), rim(8 + RIM * p)]
        near_rows = [now[1], now[0], later(before[0]), later(before[1])]
        out = []
        for i in range(RIM):
            total = taps[p][0] * near_rows[1 - i]
            for lag in range(1, tap_count):
                total = total + taps[p][lag] * near_rows[1 - i + lag]
            out.append(total)
        return out

    query_rim, key_rim, value_rim = (rim_feature(p) for p in range(streams))
    grad_rim = [rim(RIM * streams), rim(RIM * streams + 1)]

    def collect(k, rims):
        for s in range(n):
            buf[s * rows : (s + 1) * rows, :] = decode(xr[k, s].astype(f32))
        for i in range(RIM):
            buf[pl.ds(i, n, stride=rows), :] = rims[i]

    for copy in filter_passed:
        copy.wait()
    for s in range(n):
        packed = jnp.concatenate([fr[k, s] for k in range(m)], axis=0)
        for q in range(reps):
            at = s * rows + q * part
            buf[at : at + part, :] = group_sum(jnp.where(grp == q, packed, 0.0), reps)
    filt_e, filt_o = split()
    fetched.wait()

    @pl.loop(0, half // chunk)
    def _(i):
        at = pl.ds(pl.multiple_of(i * chunk, chunk), chunk)
        weight = jnp.where(row_of((chunk, LANES)) + i * chunk == 0, 1.0 / tokens, 2.0 / tokens)
        for k, value in enumerate(spectra(at)):
            fsp[k, at, :] = value * weight

    for copy in first:
        copy.wait()
    collect(0, [grad_rim[i] * query_rim[i] for i in range(RIM)])
    grad_e, grad_o = split()

    @pl.loop(0, half // chunk)
    def _(i):
        at = pl.ds(pl.multiple_of(i * chunk, chunk), chunk)
        low = pl.ds(pl.multiple_of(half + i * chunk, chunk), chunk)
        ge, te, go, to = spectra(at)
        for k, value in enumerate((ge, te, go, to)):
            gsp[k, at, :] = value
        fe, se, fo, so = (fsp[k, at, :] for k in range(4))
        store_products(
            at, low,
            fe * ge + fo * go + se * te + so * to,
            fe * te + fo * to - se * ge - so * go,
            fe * go + fo * ge + se * to + so * te,
            fe * to + fo * te - se * go - so * ge,
        )

    back_sent, back_rim = return_layout(
        0, (filt_e * grad_e + filt_o * grad_o) * (1.0 / tokens),
        (filt_e * grad_o - filt_o * grad_e) * (1.0 / tokens),
    )
    back_rims_sent = return_rims(
        0, [[back_rim[i] * value_rim[i] for i in range(RIM)], [back_rim[i] * key_rim[i] for i in range(RIM)]]
    )

    for copy in second:
        copy.wait()
    collect(1, [key_rim[i] * value_rim[i] for i in range(RIM)])
    mixed_e, mixed_o = split()

    @pl.loop(0, half // chunk)
    def _(i):
        at = pl.ds(pl.multiple_of(i * chunk, chunk), chunk)
        low = pl.ds(pl.multiple_of(half + i * chunk, chunk), chunk)
        he, ye, ho, yo = spectra(at)
        fe, se, fo, so = (fsp[k, at, :] for k in range(4))
        store_products(
            at, low,
            fe * he + fo * ho - se * ye - so * yo,
            fe * ye + fo * yo + se * he + so * ho,
            fe * ho + fo * he - se * yo - so * ye,
            fe * yo + fo * ye + se * ho + so * he,
        )
        weight = jnp.where(row_of((chunk, LANES)) + i * chunk == 0, 1.0 / tokens, 2.0 / tokens)
        ge, te, go, to = (gsp[k, at, :] for k in range(4))
        gsp[0, at, :] = (ge * he + go * ho + te * ye + to * yo) * weight
        gsp[1, at, :] = (te * he + to * ho - ge * ye - go * yo) * weight
        gsp[2, at, :] = (ge * ho + go * he + te * yo + to * ye) * weight
        gsp[3, at, :] = (te * ho + to * he - ge * yo - go * ye) * weight

    conv_sent, conv_rim = return_layout(
        1, (filt_e * mixed_e - filt_o * mixed_o) * (1.0 / tokens),
        (filt_e * mixed_o + filt_o * mixed_e) * (1.0 / tokens),
    )
    conv_rims_sent = return_rims(1, [[conv_rim[i] * grad_rim[i] for i in range(RIM)]])

    @pl.loop(0, half // chunk)
    def _(i):
        at = pl.ds(pl.multiple_of(i * chunk, chunk), chunk)
        low = pl.ds(pl.multiple_of(half + i * chunk, chunk), chunk)
        store_products(at, low, gsp[0, at, :], gsp[1, at, :], gsp[2, at, :], gsp[3, at, :])

    end_e = (grad_e * mixed_e + grad_o * mixed_o) * (1.0 / tokens)
    end_o = (grad_o * mixed_e - grad_e * mixed_o) * (1.0 / tokens)
    for c in range(half // chunk):
        even, odd = inverse(pl.ds(c * chunk, chunk), end_e, end_o)
        buf[pl.ds(2 * c * chunk, chunk, stride=2), :] = even
        buf[pl.ds(2 * c * chunk + 1, chunk, stride=2), :] = odd
    for s in range(n):
        packed = jnp.zeros((part, LANES), f32)
        for q in range(reps):
            at = s * rows + q * part
            packed = jnp.where(grp == q, group_sum(buf[at : at + part, :], reps), packed)
        for k in range(m):
            lgs[k, s] = packed[k * share : (k + 1) * share]
    long_parts = spread(1, lambda peer: lgs.at[peer], lgc.at[mine])
    lgc[mine] = lgs[mine]

    def own_rims(kind, h, r):
        line = jnp.zeros((8, LANES), f32)
        for g in range(reps):
            at = (h * reps + g) * 8
            moved = turn(backr[kind, at : at + 8, :], (g - r) * width, 1)
            line = jnp.where(lane_group(8, width) == g, moved, line)
        return line

    def own_codes(kind, h):
        return dot(jnp.concatenate([igr[kind, h * reps + g] for g in range(reps)], axis=1), sw_ref[...])

    def finish(p, at, grads, own, after):
        row8 = row_of((8, LANES))
        first_rows = jnp.where(row8 == 0, own[0:1], jnp.where(row8 == 1, own[1:2], grads[:8]))
        grads = jnp.concatenate([first_rows, grads[8:]], axis=0)
        one, two = pltpu.roll(grads, rows - 1, 0), pltpu.roll(grads, rows - 2, 0)
        last = jnp.where(row8 == 7, after[0:1], one[rows - 8 :])
        one = jnp.concatenate([one[: rows - 8], last], axis=0)
        last = jnp.where(row8 == 7, after[1:2], jnp.where(row8 == 6, after[0:1], two[rows - 8 :]))
        two = jnp.concatenate([two[: rows - 8], last], axis=0)
        x = x_ref[p, :, at].astype(f32)
        total, lines = None, []
        for lag, value in enumerate((grads, one, two)):
            term = tp_ref[p, lag : lag + 1, at] * value
            total = term if total is None else total + term
            lines.append(jnp.sum(x * value, axis=0, keepdims=True) * (1.0 / math.sqrt(tokens)))
        out_ref[p, :, at] = total.astype(bf16)
        return lines

    for copy in back_sent:
        copy.wait()
    for copy in back_rims_sent:
        copy.wait()
    ts[...] = jnp.zeros_like(ts)
    for h in range(tiles):
        moved = own_codes(0, h)
        for r in range(reps):
            at = place(r, h)
            grads = decode(moved[:, r * LANES : (r + 1) * LANES])
            edge = own_rims(0, h, r)
            for p, other in ((1, vf), (2, kf)):
                k = RIM * (p - 1)
                lines = finish(
                    p, at, grads * other[:, at], edge[k : k + RIM], edge[k + 4 : k + 4 + RIM]
                )
                for lag in range(tap_count):
                    ts[r * tiles + h, tap_count * (p - 1) + lag : tap_count * (p - 1) + lag + 1, :] = lines[lag]
    taps_parts = ship(8, lambda peer: ts.at[peer], tr.at[me])
    tr[me] = ts[me]
    for copy in long_parts:
        copy.wait()
    summed = lgc[0]
    for k in range(1, m):
        summed = summed + lgc[k]
    lsum[...] = summed
    long_sent = ship(12, lambda peer: lsum.at[peer], lgr.at[me])
    lgr[me] = lsum[me]
    for copy in taps_parts:
        copy.wait()
    summed = tr[0]
    for s in range(1, n):
        summed = summed + tr[s]
    tsum[...] = summed
    taps_sent = ship(9, lambda peer: tsum, tg.at[me])
    tg[me] = tsum[...]
    for copy in long_sent:
        copy.wait()
    per = n // m
    chan_sent = spread(2, lambda peer: lgr.at[pl.ds(peer * per, per)], l2.at[mine])
    l2[mine] = lgr[pl.ds(mine * per, per)]

    for copy in conv_sent:
        copy.wait()
    for copy in conv_rims_sent:
        copy.wait()
    us[...] = jnp.zeros_like(us)
    query_sent = []
    for h in range(tiles):
        moved = own_codes(1, h)
        for r in range(reps):
            at = place(r, h)
            grads = decode(moved[:, r * LANES : (r + 1) * LANES]) * og_ref[:, at].astype(f32)
            edge = own_rims(1, h, r)
            lines = finish(0, at, grads, edge[:RIM], edge[RIM : 2 * RIM])
            for lag in range(tap_count):
                us[h, tap_count * r + lag : tap_count * r + lag + 1, :] = lines[lag]
        query_sent.append(ship(10 + h, lambda peer: us.at[h], ug.at[h, me]))
        ug[h, me] = us[h]
    for copy in chan_sent:
        copy.wait()
    sources = [jnp.concatenate([l2[q, k] for q in range(m)], axis=0) for k in range(per)]
    lines = []
    for q in range(reps):
        line = jnp.zeros((part, LANES), f32)
        for k in range(per):
            line = jnp.where(grp == k, turn(sources[k], (k - q) * width, 1), line)
        lines.append(line)
    lo_ref[...] = jnp.concatenate(lines, axis=0).T[: per * width]
    for copy in taps_sent:
        copy.wait()
    for t in range(n):
        for p in (1, 2):
            to_ref[p, :, t * LANES : (t + 1) * LANES] = tg[t, tap_count * (p - 1) : tap_count * p]
    for h in range(tiles):
        for copy in query_sent[h]:
            copy.wait()
        summed = ug[h, 0]
        for s in range(1, n):
            summed = summed + ug[h, s]
        for r in range(reps):
            to_ref[0, :, place(r, h)] = summed[tap_count * r : tap_count * (r + 1)]


def whole_specs(count):
    return [pl.BlockSpec(memory_space=pltpu.VMEM)] * count


def half_tables(tokens):
    half = tokens // 2
    freq, step = np.arange(half)[:, None], np.arange(half)[None, :]
    even = freq * (2 * step) % (2 * tokens) * (math.pi / tokens)
    odd = freq * (2 * step + 1) % (2 * tokens) * (math.pi / tokens)
    tables = [np.cos(even), np.sin(even), np.cos(odd), np.sin(odd), np.cos(odd).T, np.sin(odd).T]
    out = []
    for table in tables:
        high = table.astype(np.float32).astype(jnp.bfloat16)
        low = (table - high.astype(np.float64)).astype(np.float32).astype(jnp.bfloat16)
        out.append(np.stack([high, low]))
    return np.stack(out)


def fast_shards(n, m, proj_in, taps, long_filter, out_grad):
    streams, rows, channels = proj_in.shape
    groups = long_filter.shape[1]
    reps = channels // groups
    part = rows // reps
    tokens = n * rows
    half = tokens // 2
    tiles = n // reps
    f32, bf16 = jnp.float32, jnp.bfloat16
    shape, vmem = jax.ShapeDtypeStruct, pltpu.VMEM
    share = part // m
    quarters = vmem((m, n, share, LANES), f32)
    quarter = vmem((n, share, LANES), f32)
    moved = vmem((2, n, rows, LANES), bf16)
    rims = vmem((n, 16, LANES), bf16)
    features = vmem((rows, channels), f32)
    both = vmem((half, 2 * LANES), bf16)
    spectrum = vmem((4, half, LANES), f32)
    products = vmem((tokens, 2 * LANES), bf16)
    edges = vmem((2, n * 8, LANES), f32)
    lines = vmem((n, 8, LANES), f32)
    out, long_grad, tap_grad = pl.pallas_call(
        functools.partial(whole_kernel, n, m, reps),
        out_shape=(
            shape((streams, rows, channels), bf16), shape((groups // m, rows), f32), shape(taps.shape, f32),
        ),
        in_specs=whole_specs(5) + [pl.BlockSpec(memory_space=pl.ANY)],
        out_specs=whole_specs(3),
        scratch_shapes=[vmem((6, 2, half, half), bf16), vmem((16, channels), f32), rims, rims]
        + [vmem((n * 16, LANES), f32), moved, moved, features, features]
        + [vmem((n, m, share, LANES), f32), quarters, vmem((tokens, LANES), f32), both, both]
        + [spectrum, spectrum, products, products, vmem((2, half, LANES), f32)]
        + [vmem((2, 2, n // 2, rows, LANES), bf16), moved, edges, edges]
        + [quarters, quarters, quarter, quarter, vmem((m, n // m, share, LANES), f32)]
        + [lines, lines, vmem((8, LANES), f32), lines]
        + [vmem((tiles, 16, LANES), f32), vmem((tiles, n, 16, LANES), f32)]
        + [pltpu.SemaphoreType.DMA((1,)), pltpu.SemaphoreType.DMA((2, 13, n - 1))]
        + [pltpu.SemaphoreType.DMA((2, 3, m - 1))],
        compiler_params=pltpu.CompilerParams(
            collective_id=0, has_side_effects=True, vmem_limit_bytes=56 << 20
        ),
    )(
        proj_in, out_grad, long_filter, taps, swap_matrix(reps, LANES // reps), half_tables(tokens)
    )
    return (out, long_grad.T, tap_grad)


def fits(n, m, proj_in, taps, long_filter, out_grad):
    streams, rows, channels = proj_in.shape
    groups = long_filter.shape[1]
    if channels % groups or groups % n or n % m or streams != 3 or taps.shape[1] != 3:
        return False
    reps, width = channels // groups, groups // n
    if reps < 2 or reps * width != LANES or n % reps or rows % (8 * reps * m) or rows % LANES:
        return False
    if n % 8 or reps * 3 > 16:
        return False
    return n * rows <= TABLE_LIMIT and n * rows % 1024 == 0


def routed(n, m, *arrays):
    return fast_shards(n, m, *arrays) if fits(n, m, *arrays) else shards(*arrays)


def solution(mesh):
    return jax.shard_map(
        functools.partial(routed, mesh.shape["seq"], mesh.shape["chan"]),
        mesh=mesh,
        in_specs=(P(None, "seq", "chan"), P(None, None, "chan"), P("seq", None), P("seq", "chan")),
        out_specs=(P(None, "seq", "chan"), P("seq", "chan"), P(None, None, "chan")),
        check_vma=False,
    )
```

```python
import functools
import math

import jax
import jax.numpy as jnp
import numpy as np
from jax import lax
from jax.experimental import pallas as pl
from jax.experimental.pallas import tpu as pltpu
from jax.sharding import PartitionSpec as P

MESH = pl.DeviceIdType.MESH
LANES = 128
TABLE_LIMIT = 1024
LEVELS = 250.0
RIM = 2


def shifted(x, axis, by):
    devices = lax.axis_size(axis)
    pairs = [(i, i + by) for i in range(devices) if 0 <= i + by < devices]
    return lax.ppermute(x, axis, pairs)


def angle_table(left_index, right_index, period):
    product = left_index[:, None] * right_index[None, :] % period
    phase = product.astype(jnp.float32) * (2.0 * math.pi / period)
    return (jnp.cos(phase), jnp.sin(phase))


def contract(pattern, factor_table, operand):
    return jnp.einsum(pattern, factor_table, operand, precision=lax.Precision.HIGHEST)


def steps_of(count):
    return jnp.arange(count, dtype=jnp.int32)


def whole_forward(signal, seq_width):
    tok_rows, stack_count, channels = signal.shape
    period = 2 * seq_width * tok_rows
    narrow = channels // seq_width
    arrived = lax.all_to_all(signal, "seq", split_axis=2, concat_axis=0, tiled=True)
    laid = arrived.reshape(seq_width, tok_rows, stack_count, narrow).transpose(2, 3, 0, 1)
    cos_step, sin_step = angle_table(steps_of(2 * seq_width), steps_of(seq_width), 2 * seq_width)
    real_part = contract("qm,ncmj->ncqj", cos_step, laid)
    imag_part = -contract("qm,ncmj->ncqj", sin_step, laid)
    cos_turn, sin_turn = angle_table(steps_of(2 * seq_width), steps_of(tok_rows), period)
    turned_re = real_part * cos_turn + imag_part * sin_turn
    turned_im = imag_part * cos_turn - real_part * sin_turn
    cos_row, sin_row = angle_table(steps_of(tok_rows), steps_of(tok_rows), tok_rows)
    spec_re = contract("rj,ncqj->ncqr", cos_row, turned_re) + contract(
        "rj,ncqj->ncqr", sin_row, turned_im
    )
    spec_im = contract("rj,ncqj->ncqr", cos_row, turned_im) - contract(
        "rj,ncqj->ncqr", sin_row, turned_re
    )
    return (spec_re, spec_im)


def whole_inverse(spec_re, spec_im, seq_width):
    stack_count, narrow, freq_count, tok_rows = spec_re.shape
    period = 2 * seq_width * tok_rows
    cos_row, sin_row = angle_table(steps_of(tok_rows), steps_of(tok_rows), tok_rows)
    back_re = contract("rj,ncqr->ncqj", cos_row, spec_re) - contract(
        "rj,ncqr->ncqj", sin_row, spec_im
    )
    back_im = contract("rj,ncqr->ncqj", sin_row, spec_re) + contract(
        "rj,ncqr->ncqj", cos_row, spec_im
    )
    cos_turn, sin_turn = angle_table(steps_of(freq_count), steps_of(tok_rows), period)
    turned_re = back_re * cos_turn - back_im * sin_turn
    turned_im = back_re * sin_turn + back_im * cos_turn
    cos_step, sin_step = angle_table(steps_of(seq_width), steps_of(freq_count), freq_count)
    signal = contract("mq,ncqj->ncmj", cos_step, turned_re) - contract(
        "mq,ncqj->ncmj", sin_step, turned_im
    )
    signal = (
        (signal / period).transpose(2, 3, 0, 1).reshape(seq_width * tok_rows, stack_count, narrow)
    )
    return lax.all_to_all(signal, "seq", split_axis=0, concat_axis=2, tiled=True)


def member(values, index, stack_axis):
    return lax.index_in_dim(values, index, stack_axis, keepdims=False)


def shards(proj_in, taps, long_filter, out_grad):
    stream_count, tok_rows, channels = proj_in.shape
    tap_count = taps.shape[1]
    groups = long_filter.shape[1]
    seq_width = lax.axis_size("seq")
    lower_rim = shifted(proj_in[:, tok_rows - (tap_count - 1) :, :], "seq", 1)
    extended = jnp.concatenate([lower_rim, proj_in], axis=1).astype(jnp.float32)
    lagged = [
        extended[:, tap_count - 1 - lag_step : tap_count - 1 - lag_step + tok_rows, :]
        for lag_step in range(tap_count)
    ]
    featured = taps[:, 0, None, :] * lagged[0]
    for lag_step in range(1, tap_count):
        featured = featured + taps[:, lag_step, None, :] * lagged[lag_step]
    query_rows, key_rows, value_rows = (featured[0], featured[1], featured[2])
    mixed_rows = key_rows * value_rows
    upstream = out_grad.astype(jnp.float32)
    conv_grad = upstream * query_rows
    tiled_filter = jnp.tile(long_filter, (1, channels // groups))
    signals = jnp.stack([mixed_rows, conv_grad, tiled_filter], axis=1)
    data_re, data_im = whole_forward(signals, seq_width)
    stack_axis = 0
    mix_re, mix_im = (member(data_re, 0, stack_axis), member(data_im, 0, stack_axis))
    grad_re, grad_im = (member(data_re, 1, stack_axis), member(data_im, 1, stack_axis))
    filt_re, filt_im = (member(data_re, 2, stack_axis), member(data_im, 2, stack_axis))
    conv_re = filt_re * mix_re - filt_im * mix_im
    conv_im = filt_re * mix_im + filt_im * mix_re
    back_re = filt_re * grad_re + filt_im * grad_im
    back_im = filt_re * grad_im - filt_im * grad_re
    corr_re = grad_re * mix_re + grad_im * mix_im
    corr_im = grad_im * mix_re - grad_re * mix_im
    prod_re = jnp.stack([conv_re, back_re, corr_re], axis=stack_axis)
    prod_im = jnp.stack([conv_im, back_im, corr_im], axis=stack_axis)
    outputs = whole_inverse(prod_re, prod_im, seq_width)
    conv_out, mixed_grad = (outputs[:, 0], outputs[:, 1])
    filt_grad = jnp.sum(outputs[:, 2].reshape(tok_rows, channels // groups, groups), axis=1)
    long_grad = lax.psum_scatter(filt_grad, "chan", scatter_dimension=1, tiled=True)
    feature_grad = jnp.stack(
        [upstream * conv_out, mixed_grad * value_rows, mixed_grad * key_rows], axis=0
    )
    upper_rim = shifted(feature_grad[:, : tap_count - 1, :], "seq", -1)
    trailing = jnp.concatenate([feature_grad, upper_rim], axis=1)
    input_grad = taps[:, 0, None, :] * feature_grad
    for lag_step in range(1, tap_count):
        input_grad = (
            input_grad + taps[:, lag_step, None, :] * trailing[:, lag_step : lag_step + tok_rows]
        )
    partial_taps = jnp.stack(
        [jnp.sum(feature_grad * lagged[lag_step], axis=1) for lag_step in range(tap_count)], axis=1
    )
    tap_grad = lax.psum(partial_taps, "seq") / math.sqrt(seq_width * tok_rows)
    return (input_grad.astype(jnp.bfloat16), long_grad, tap_grad)


def greet(axis_sizes):
    barrier = pltpu.get_barrier_semaphore()
    for axis, size in axis_sizes:
        me = lax.axis_index(axis)
        for j in range(1, size):
            pl.semaphore_signal(
                barrier, inc=1, device_id={axis: lax.rem(me + j, size)}, device_id_type=MESH
            )


def welcome(sizes):
    pl.semaphore_wait(pltpu.get_barrier_semaphore(), sum(size - 1 for size in sizes))


def swap_matrix(reps, width):
    side = reps * LANES
    row, col = np.arange(side)[:, None], np.arange(side)[None, :]
    outer, inner, rest = row // LANES, (row % LANES) // width, row % width
    return (inner * LANES + outer * width + rest == col).astype(jnp.bfloat16)


def lane_group(rows, width):
    return lax.broadcasted_iota(jnp.int32, (rows, LANES), 1) // width


def row_of(shape):
    return lax.broadcasted_iota(jnp.int32, shape, 0)


def turn(x, shift, axis):
    shift = shift % x.shape[axis]
    return x if shift == 0 else pltpu.roll(x, shift, axis)


def halves(x):
    high = x.astype(jnp.bfloat16)
    return high, (x - high.astype(jnp.float32)).astype(jnp.bfloat16)


def later(x):
    return jnp.where(row_of(x.shape) < 1, 0.0, pltpu.roll(x, 1, 0))


def sooner(x):
    rows = x.shape[0]
    return jnp.where(row_of(x.shape) >= rows - 1, 0.0, pltpu.roll(x, rows - 1, 0))


def group_sum(x, reps):
    step = LANES // reps
    if reps & (reps - 1):
        return sum((turn(x, r * step, 1) for r in range(1, reps)), x)
    while step < LANES:
        x = x + turn(x, step, 1)
        step *= 2
    return x


def encode(x):
    size = jnp.abs(x)
    first = jnp.where(row_of((8, LANES)) < RIM, 0.0, size[:8])
    top = jnp.max(jnp.concatenate([first, size[8:]], axis=0), axis=0, keepdims=True)
    scale = jnp.maximum(top * (1.0 + 2.0**-7), 1e-30).astype(jnp.bfloat16).astype(jnp.float32)
    level = jnp.exp2(size * (LEVELS / scale) - 0.5 * LEVELS)
    level = jnp.where(x < 0.0, -level, level)
    first = jnp.where(row_of((8, LANES)) < RIM, scale, level[:8])
    return jnp.concatenate([first, level[8:]], axis=0).astype(jnp.bfloat16)


def decode(code):
    scale = code[:1]
    size = (jnp.log(jnp.abs(code)) * (1.0 / (math.log(2.0) * LEVELS)) + 0.5) * scale
    return jnp.where(code < 0.0, -size, size)


def dot(left, right):
    return jnp.dot(left, right, preferred_element_type=jnp.float32)


def three(high, low, x_high, x_low):
    return dot(high, x_high) + (dot(high, x_low) + dot(low, x_high))


def paired(high, low, both):
    wide = dot(high, both)
    return wide[:, :LANES] + (wide[:, LANES:] + dot(low, both[:, :LANES]))


def alternating(count):
    return jnp.where(row_of((count, LANES)) % 2 == 0, 1.0, -1.0)


def whole_kernel(
    n, m, reps, x_hbm, og_hbm, lf_hbm, tp_hbm, sw_hbm, tb_hbm, out_ref, lo_ref, to_ref,
    x_ref, og_ref, lf_ref, tp_ref, sw_ref, tb, ex, es, er, exf, xs, xr, kf, vf, fs, fr, buf, both_e, both_o, fsp, gsp, pq_e, pq_o, eh, el, oh, ol,
    half_out, corr, codes, igr, back, backr, lgs, lgc, lsum, lgr, l2, ts, tr, tsum, tg, us, ug, lsem, sems, csems,
):
    me, mine = lax.axis_index("seq"), lax.axis_index("chan")
    width = LANES // reps
    streams, rows, _ = x_ref.shape
    tap_count = tp_ref.shape[1]
    tokens = n * rows
    half = tokens // 2
    near = n // 2
    part = rows // reps
    share = part // m
    tiles = n // reps
    f32, bf16 = jnp.float32, jnp.bfloat16
    pairs = [
        (lf_hbm, lf_ref), (og_hbm, og_ref), (x_hbm.at[0], x_ref.at[0]), (tp_hbm, tp_ref),
        (sw_hbm, sw_ref), (x_hbm.at[1], x_ref.at[1]), (x_hbm.at[2], x_ref.at[2]), (tb_hbm, tb),
    ]
    fetched = [pltpu.make_async_copy(*pair, lsem.at[i]) for i, pair in enumerate(pairs)]
    for copy in fetched:
        copy.start()
    grp = lane_group(part, width)
    greet([("seq", n), ("chan", m)])
    fetched[0].wait()

    def remote(kind, slot, source, target, peer):
        copy = pltpu.make_async_remote_copy(
            src_ref=source, dst_ref=target, send_sem=sems.at[0, kind, slot],
            recv_sem=sems.at[1, kind, slot], device_id={"seq": peer}, device_id_type=MESH,
        )
        copy.start()
        return copy

    def ship(kind, source, target):
        return [
            remote(kind, j - 1, source(lax.rem(me + j, n)), target, lax.rem(me + j, n))
            for j in sorted(range(1, n), key=lambda j: abs(2 * j - n))
        ]

    def spread(kind, source, target):
        copies = []
        for j in range(1, m):
            peer = lax.rem(mine + j, m)
            copy = pltpu.make_async_remote_copy(
                src_ref=source(peer), dst_ref=target, send_sem=csems.at[0, kind, j - 1],
                recv_sem=csems.at[1, kind, j - 1], device_id={"chan": peer}, device_id_type=MESH,
            )
            copy.start()
            copies.append(copy)
        return copies

    def place(r, h):
        return pl.ds(pl.multiple_of((r * tiles + h) * LANES, LANES), LANES)

    def feature(p, at):
        x = x_ref[p, :, at].astype(f32)
        total = tp_ref[p, 0:1, at] * x
        for lag in range(1, tap_count):
            total = total + tp_ref[p, lag : lag + 1, at] * pltpu.roll(x, lag, 0)
        return total

    def send_layout(pieces, place_at):
        moved = dot(jnp.concatenate(pieces, axis=1), sw_ref[...]).astype(bf16)
        for g in range(reps):
            place_at(g)[...] = moved[:, g * LANES : (g + 1) * LANES]

    for s in range(n):
        base = (s // reps) * LANES
        packed = jnp.zeros((part, LANES), f32)
        for q in range(reps):
            tile = lf_ref[q * part : (q + 1) * part, base : base + LANES]
            packed = jnp.where(grp == q, turn(tile, (q - s % reps) * width, 1), packed)
        fs[s] = packed.reshape(m, share, LANES)
    for copy in fetched[1:-1]:
        copy.wait()
    welcome([n, m])
    filter_sent = ship(0, lambda peer: fs.at[peer, mine], fr.at[mine, me])
    ex[...] = jnp.zeros_like(ex)
    for p in range(streams):
        ex[RIM * p : RIM * (p + 1), :] = x_ref[p, :16, :].astype(f32)[:RIM]
        ex[8 + RIM * p : 8 + RIM * (p + 1), :] = x_ref[p, rows - 16 :, :].astype(f32)[16 - RIM :]
    ex[RIM * streams : RIM * (streams + 1), :] = og_ref[:16, :].astype(f32)[:RIM]
    for h in range(tiles):
        send_layout(
            [ex[:, place(r, h)].astype(bf16) for r in range(reps)], lambda g: es.at[h * reps + g]
        )
    rims_sent = ship(1, lambda peer: es.at[peer], er.at[me])
    side = me // near

    def halves_of_ship(kind, plane, piece):
        copies = []
        for step in range(2):
            which = (1 - side) if step == 0 else side
            for k in range(near // reps):
                h = which * (near // reps) + k
                send_layout([piece(place(r, h)) for r in range(reps)], lambda g: xs.at[plane, h * reps + g])
            for i in range(step, near):
                peer = which * near + lax.rem(me + i, near)
                copies.append(
                    remote(kind, step * near + i - step, xs.at[plane, peer], xr.at[plane, me], peer)
                )
        return copies

    def mixed_piece(at):
        key, value = feature(1, at), feature(2, at)
        kf[:, at], vf[:, at] = key, value
        return encode(key * value)

    first = halves_of_ship(2, 0, lambda at: encode(og_ref[:, at].astype(f32) * feature(0, at)))
    fr[mine, me] = fs[me, mine]
    for copy in filter_sent:
        copy.wait()
    filter_passed = spread(0, lambda peer: fr.at[mine], fr.at[mine])
    second = halves_of_ship(3, 1, mixed_piece)
    er[me] = es[me]
    xr[0, me] = xs[0, me]
    xr[1, me] = xs[1, me]

    taps = []
    home, slot = me // reps, lax.rem(me, reps)
    for p in range(streams):
        mixed_taps = jnp.zeros((tap_count, LANES), f32)
        for r in range(reps):
            at = pl.multiple_of((r * tiles + home) * LANES, LANES)
            tile = tp_ref[p, :, pl.ds(at, LANES)]
            shift = lax.rem((r + reps - slot) * width, LANES)
            mixed_taps = jnp.where(
                lane_group(tap_count, width) == r, pltpu.roll(tile, shift, 1), mixed_taps
            )
        taps.append([mixed_taps[i : i + 1] for i in range(tap_count)])

    def split():
        ends = []
        for part_of, both in ((0, both_e), (1, both_o)):
            values = buf[pl.ds(part_of, half, stride=2), :]
            both[:, :LANES], both[:, LANES:] = halves(values)
            ends.append(jnp.sum(alternating(half) * values, axis=0, keepdims=True))
        return ends

    chunk = min(256, half)

    def spectra(at):
        return [
            paired(tb[table, 0, at, :], tb[table, 1, at, :], both[...])
            for table, both in ((0, both_e), (1, both_e), (2, both_o), (3, both_o))
        ]

    def store_products(at, low, even_cos, even_sin, odd_cos, odd_sin):
        pq_e[at, :LANES], pq_e[at, LANES:] = halves(even_cos)
        pq_e[low, :LANES], pq_e[low, LANES:] = halves(even_sin)
        pq_o[at, :LANES], pq_o[at, LANES:] = halves(odd_cos)
        pq_o[low, :LANES], pq_o[low, LANES:] = halves(odd_sin)

    def inverse(at, end_e, end_o):
        even = paired(tb[0, 0, at, :], tb[0, 1, at, :], pq_e[:half])
        even = even + paired(tb[1, 0, at, :], tb[1, 1, at, :], pq_e[half:])
        odd = paired(tb[4, 0, at, :], tb[4, 1, at, :], pq_o[:half])
        odd = odd + paired(tb[5, 0, at, :], tb[5, 1, at, :], pq_o[half:])
        sign = alternating(chunk)
        return [even + sign * end_e], [odd + sign * end_o]

    def inverse_both(at, end_e, end_o):
        even = three(tb[0, 0, at, :], tb[0, 1, at, :], eh[:half], el[:half])
        even = even + three(tb[1, 0, at, :], tb[1, 1, at, :], eh[half:], el[half:])
        odd = three(tb[4, 0, at, :], tb[4, 1, at, :], oh[:half], ol[:half])
        odd = odd + three(tb[5, 0, at, :], tb[5, 1, at, :], oh[half:], ol[half:])
        sign = alternating(chunk)
        lanes = (slice(0, LANES), slice(LANES, 2 * LANES))
        return tuple(
            [value[:, lane] + sign * end[k] for k, lane in enumerate(lanes)]
            for value, end in ((even, end_e), (odd, end_o))
        )

    def return_layout(kind, inverse_of, end_e, end_o, between=lambda: None):
        copies = []
        for step in range(2):
            which = (1 - side) if step == 0 else side
            for c in range(half // 2 // chunk):
                at = pl.ds(pl.multiple_of(which * (half // 2) + c * chunk, chunk), chunk)
                for offset, values in enumerate(inverse_of(at, end_e, end_o)):
                    for value, place_of in zip(values, (half_out, corr)):
                        place_of[step, pl.ds(2 * c * chunk + offset, chunk, stride=2), :] = value
            for i in range(near):
                codes[kind, step, i] = encode(half_out[step, i * rows : (i + 1) * rows, :])
            if step == 1:
                between()
            for i in range(step, near):
                inner = lax.rem(me + i, near)
                copies.append(
                    remote(
                        4 + 2 * kind, step * near + i - step, codes.at[kind, step, inner],
                        igr.at[kind, me], which * near + inner,
                    )
                )
        igr[kind, me] = codes[kind, 1, lax.rem(me, near)]
        rims = []
        for i in range(RIM):
            far_rows = half_out[0, pl.ds(i, near, stride=rows), :]
            near_rows = half_out[1, pl.ds(i, near, stride=rows), :]
            low = jnp.where(side == 0, near_rows, far_rows)
            high = jnp.where(side == 0, far_rows, near_rows)
            rims.append(jnp.concatenate([low, high], axis=0))
        return copies, rims

    def return_rims(kind, grads):
        if len(grads) == 1:
            back[kind, ...] = jnp.zeros_like(back[kind])
        for k, pair in enumerate(grads):
            for i in range(RIM):
                back[kind, pl.ds(RIM * k + i, n, stride=8), :] = pair[i]
                back[kind, pl.ds(RIM * (k + len(grads)) + i, n, stride=8), :] = sooner(pair[i])
        mine_at = pl.ds(pl.multiple_of(me * 8, 8), 8)
        backr[kind, mine_at, :] = back[kind, mine_at, :]
        return ship(
            5 + 2 * kind, lambda peer: back.at[kind, pl.ds(pl.multiple_of(peer * 8, 8), 8)],
            backr.at[kind, mine_at],
        )

    for copy in rims_sent:
        copy.wait()
    exf[...] = er[...].reshape(n * 16, LANES).astype(f32)

    def rim(i):
        return exf[pl.ds(i, n, stride=16), :]

    def rim_feature(p):
        now, before = [rim(RIM * p), rim(RIM * p + 1)], [rim(8 + RIM * p + 1), rim(8 + RIM * p)]
        near_rows = [now[1], now[0], later(before[0]), later(before[1])]
        out = []
        for i in range(RIM):
            total = taps[p][0] * near_rows[1 - i]
            for lag in range(1, tap_count):
                total = total + taps[p][lag] * near_rows[1 - i + lag]
            out.append(total)
        return out

    query_rim, key_rim, value_rim = (rim_feature(p) for p in range(streams))
    grad_rim = [rim(RIM * streams), rim(RIM * streams + 1)]

    def collect(k, rims):
        for s in range(n):
            buf[s * rows : (s + 1) * rows, :] = decode(xr[k, s].astype(f32))
        for i in range(RIM):
            buf[pl.ds(i, n, stride=rows), :] = rims[i]

    for copy in filter_passed:
        copy.wait()
    for s in range(n):
        packed = jnp.concatenate([fr[k, s] for k in range(m)], axis=0)
        for q in range(reps):
            at = s * rows + q * part
            buf[at : at + part, :] = group_sum(jnp.where(grp == q, packed, 0.0), reps)
    filt_e, filt_o = split()
    fetched[-1].wait()

    @pl.loop(0, half // chunk)
    def _(i):
        at = pl.ds(pl.multiple_of(i * chunk, chunk), chunk)
        weight = jnp.where(row_of((chunk, LANES)) + i * chunk == 0, 1.0 / tokens, 2.0 / tokens)
        for k, value in enumerate(spectra(at)):
            fsp[k, at, :] = value * weight

    for copy in first:
        copy.wait()
    collect(0, [grad_rim[i] * query_rim[i] for i in range(RIM)])
    grad_e, grad_o = split()

    @pl.loop(0, half // chunk)
    def _(i):
        at = pl.ds(pl.multiple_of(i * chunk, chunk), chunk)
        low = pl.ds(pl.multiple_of(half + i * chunk, chunk), chunk)
        ge, te, go, to = spectra(at)
        for k, value in enumerate((ge, te, go, to)):
            gsp[k, at, :] = value
        fe, se, fo, so = (fsp[k, at, :] for k in range(4))
        store_products(
            at, low,
            fe * ge + fo * go + se * te + so * to,
            fe * te + fo * to - se * ge - so * go,
            fe * go + fo * ge + se * to + so * te,
            fe * to + fo * te - se * go - so * ge,
        )

    back_sent, back_rim = return_layout(
        0, inverse, (filt_e * grad_e + filt_o * grad_o) * (1.0 / tokens),
        (filt_e * grad_o - filt_o * grad_e) * (1.0 / tokens),
    )
    back_rims_sent = return_rims(
        0, [[back_rim[i] * value_rim[i] for i in range(RIM)], [back_rim[i] * key_rim[i] for i in range(RIM)]]
    )

    for copy in second:
        copy.wait()
    collect(1, [key_rim[i] * value_rim[i] for i in range(RIM)])
    mixed_e, mixed_o = split()

    @pl.loop(0, half // chunk)
    def _(i):
        at = pl.ds(pl.multiple_of(i * chunk, chunk), chunk)
        low = pl.ds(pl.multiple_of(half + i * chunk, chunk), chunk)
        he, ye, ho, yo = spectra(at)
        fe, se, fo, so = (fsp[k, at, :] for k in range(4))
        ge, te, go, to = (gsp[k, at, :] for k in range(4))
        weight = jnp.where(row_of((chunk, LANES)) + i * chunk == 0, 1.0 / tokens, 2.0 / tokens)

        def put(high, low_part, rows_at, conv, cross):
            high[rows_at, :LANES], low_part[rows_at, :LANES] = halves(conv)
            high[rows_at, LANES:], low_part[rows_at, LANES:] = halves(cross * weight)

        put(
            eh, el, at, fe * he + fo * ho - se * ye - so * yo,
            ge * he + go * ho + te * ye + to * yo,
        )
        put(
            eh, el, low, fe * ye + fo * yo + se * he + so * ho,
            te * he + to * ho - ge * ye - go * yo,
        )
        put(
            oh, ol, at, fe * ho + fo * he - se * yo - so * ye,
            ge * ho + go * he + te * yo + to * ye,
        )
        put(
            oh, ol, low, fe * yo + fo * ye + se * ho + so * he,
            te * ho + to * he - ge * yo - go * ye,
        )

    long_parts = []

    def filter_terms():
        for s in range(n):
            packed = jnp.zeros((part, LANES), f32)
            for q in range(reps):
                at = s % near * rows + q * part
                step = jnp.where(side == s // near, 1, 0)
                packed = jnp.where(grp == q, group_sum(corr[step, at : at + part, :], reps), packed)
            for k in range(m):
                lgs[k, s] = packed[k * share : (k + 1) * share]
        long_parts.extend(spread(1, lambda peer: lgs.at[peer], lgc.at[mine]))
        lgc[mine] = lgs[mine]

    inv = 1.0 / tokens
    conv_sent, conv_rim = return_layout(
        1, inverse_both,
        ((filt_e * mixed_e - filt_o * mixed_o) * inv, (grad_e * mixed_e + grad_o * mixed_o) * inv),
        ((filt_e * mixed_o + filt_o * mixed_e) * inv, (grad_o * mixed_e - grad_e * mixed_o) * inv),
        filter_terms,
    )
    conv_rims_sent = return_rims(1, [[conv_rim[i] * grad_rim[i] for i in range(RIM)]])

    def own_rims(kind, h, r):
        line = jnp.zeros((8, LANES), f32)
        for g in range(reps):
            at = (h * reps + g) * 8
            moved = turn(backr[kind, at : at + 8, :], (g - r) * width, 1)
            line = jnp.where(lane_group(8, width) == g, moved, line)
        return line

    def own_codes(kind, h):
        return dot(jnp.concatenate([igr[kind, h * reps + g] for g in range(reps)], axis=1), sw_ref[...])

    def finish(p, at, grads, own, after):
        row8 = row_of((8, LANES))
        first_rows = jnp.where(row8 == 0, own[0:1], jnp.where(row8 == 1, own[1:2], grads[:8]))
        grads = jnp.concatenate([first_rows, grads[8:]], axis=0)
        one, two = pltpu.roll(grads, rows - 1, 0), pltpu.roll(grads, rows - 2, 0)
        last = jnp.where(row8 == 7, after[0:1], one[rows - 8 :])
        one = jnp.concatenate([one[: rows - 8], last], axis=0)
        last = jnp.where(row8 == 7, after[1:2], jnp.where(row8 == 6, after[0:1], two[rows - 8 :]))
        two = jnp.concatenate([two[: rows - 8], last], axis=0)
        x = x_ref[p, :, at].astype(f32)
        total, lines = None, []
        for lag, value in enumerate((grads, one, two)):
            term = tp_ref[p, lag : lag + 1, at] * value
            total = term if total is None else total + term
            lines.append(jnp.sum(x * value, axis=0, keepdims=True) * (1.0 / math.sqrt(tokens)))
        out_ref[p, :, at] = total.astype(bf16)
        return lines

    for copy in back_sent:
        copy.wait()
    for copy in back_rims_sent:
        copy.wait()
    ts[...] = jnp.zeros_like(ts)
    for h in range(tiles):
        moved = own_codes(0, h)
        for r in range(reps):
            at = place(r, h)
            grads = decode(moved[:, r * LANES : (r + 1) * LANES])
            edge = own_rims(0, h, r)
            for p, other in ((1, vf), (2, kf)):
                k = RIM * (p - 1)
                lines = finish(
                    p, at, grads * other[:, at], edge[k : k + RIM], edge[k + 4 : k + 4 + RIM]
                )
                for lag in range(tap_count):
                    ts[r * tiles + h, tap_count * (p - 1) + lag : tap_count * (p - 1) + lag + 1, :] = lines[lag]
    taps_parts = ship(8, lambda peer: ts.at[peer], tr.at[me])
    tr[me] = ts[me]
    for copy in long_parts:
        copy.wait()
    summed = lgc[0]
    for k in range(1, m):
        summed = summed + lgc[k]
    lsum[...] = summed
    long_sent = ship(12, lambda peer: lsum.at[peer], lgr.at[me])
    lgr[me] = lsum[me]
    for copy in conv_sent:
        copy.wait()
    for copy in conv_rims_sent:
        copy.wait()
    us[...] = jnp.zeros_like(us)
    query_sent = []
    for h in range(tiles):
        moved = own_codes(1, h)
        for r in range(reps):
            at = place(r, h)
            grads = decode(moved[:, r * LANES : (r + 1) * LANES]) * og_ref[:, at].astype(f32)
            edge = own_rims(1, h, r)
            lines = finish(0, at, grads, edge[:RIM], edge[RIM : 2 * RIM])
            for lag in range(tap_count):
                us[h, tap_count * r + lag : tap_count * r + lag + 1, :] = lines[lag]
        query_sent.append(ship(10 + h, lambda peer: us.at[h], ug.at[h, me]))
        ug[h, me] = us[h]
    for copy in taps_parts:
        copy.wait()
    summed = tr[0]
    for s in range(1, n):
        summed = summed + tr[s]
    tsum[...] = summed
    taps_sent = ship(9, lambda peer: tsum, tg.at[me])
    tg[me] = tsum[...]
    for copy in long_sent:
        copy.wait()
    per = n // m
    chan_sent = spread(2, lambda peer: lgr.at[pl.ds(peer * per, per)], l2.at[mine])
    l2[mine] = lgr[pl.ds(mine * per, per)]

    for copy in chan_sent:
        copy.wait()
    sources = [jnp.concatenate([l2[q, k] for q in range(m)], axis=0) for k in range(per)]
    lines = []
    for q in range(reps):
        line = jnp.zeros((part, LANES), f32)
        for k in range(per):
            line = jnp.where(grp == k, turn(sources[k], (k - q) * width, 1), line)
        lines.append(line)
    lo_ref[...] = jnp.concatenate(lines, axis=0).T[: per * width]
    for copy in taps_sent:
        copy.wait()
    for t in range(n):
        for p in (1, 2):
            to_ref[p, :, t * LANES : (t + 1) * LANES] = tg[t, tap_count * (p - 1) : tap_count * p]
    for h in range(tiles):
        for copy in query_sent[h]:
            copy.wait()
        summed = ug[h, 0]
        for s in range(1, n):
            summed = summed + ug[h, s]
        for r in range(reps):
            to_ref[0, :, place(r, h)] = summed[tap_count * r : tap_count * (r + 1)]


def hand_over(out_from, long_from, tap_from, out_to, long_to, tap_to, out_at, long_at, tap_at, sem):
    steps = [(out_from.at[p], out_at.at[p], out_to.at[p]) for p in range(out_from.shape[0])]
    steps += [(tap_from, tap_at, tap_to), (long_from, long_at, long_to)]
    inward = [pltpu.make_async_copy(a, b, sem.at[0, i]) for i, (a, b, _) in enumerate(steps)]
    outward = [pltpu.make_async_copy(b, c, sem.at[1, i]) for i, (_, b, c) in enumerate(steps)]
    for copy in inward:
        copy.start()
    for first, then in zip(inward, outward):
        first.wait()
        then.start()
    for copy in outward:
        copy.wait()


def whole_specs(count):
    return [pl.BlockSpec(memory_space=pltpu.VMEM)] * count


def half_tables(tokens):
    half = tokens // 2
    freq, step = np.arange(half)[:, None], np.arange(half)[None, :]
    even = freq * (2 * step) % (2 * tokens) * (math.pi / tokens)
    odd = freq * (2 * step + 1) % (2 * tokens) * (math.pi / tokens)
    tables = [np.cos(even), np.sin(even), np.cos(odd), np.sin(odd), np.cos(odd).T, np.sin(odd).T]
    out = []
    for table in tables:
        high = table.astype(np.float32).astype(jnp.bfloat16)
        low = (table - high.astype(np.float64)).astype(np.float32).astype(jnp.bfloat16)
        out.append(np.stack([high, low]))
    return np.stack(out)


def fast_shards(n, m, proj_in, taps, long_filter, out_grad):
    streams, rows, channels = proj_in.shape
    groups = long_filter.shape[1]
    reps = channels // groups
    part = rows // reps
    tokens = n * rows
    half = tokens // 2
    tiles = n // reps
    f32, bf16 = jnp.float32, jnp.bfloat16
    shape, vmem = jax.ShapeDtypeStruct, pltpu.VMEM
    share = part // m
    quarters = vmem((m, n, share, LANES), f32)
    quarter = vmem((n, share, LANES), f32)
    moved = vmem((2, n, rows, LANES), bf16)
    rims = vmem((n, 16, LANES), bf16)
    features = vmem((rows, channels), f32)
    both = vmem((half, 2 * LANES), bf16)
    spectrum = vmem((4, half, LANES), f32)
    products = vmem((tokens, 2 * LANES), bf16)
    edges = vmem((2, n * 8, LANES), f32)
    lines = vmem((n, 8, LANES), f32)
    out, long_grad, tap_grad = pl.pallas_call(
        functools.partial(whole_kernel, n, m, reps),
        out_shape=(
            shape((streams, rows, channels), bf16), shape((groups // m, rows), f32), shape(taps.shape, f32),
        ),
        in_specs=[pl.BlockSpec(memory_space=pl.ANY)] * 6,
        out_specs=whole_specs(3),
        scratch_shapes=[vmem(proj_in.shape, bf16), vmem(out_grad.shape, bf16)]
        + [vmem(long_filter.shape, f32), vmem(taps.shape, f32), vmem((reps * LANES, reps * LANES), bf16)]
        + [vmem((6, 2, half, half), bf16), vmem((16, channels), f32), rims, rims]
        + [vmem((n * 16, LANES), f32), moved, moved, features, features]
        + [vmem((n, m, share, LANES), f32), quarters, vmem((tokens, LANES), f32), both, both]
        + [spectrum, spectrum] + [products] * 6 + [vmem((2, half, LANES), f32)] * 2
        + [vmem((2, 2, n // 2, rows, LANES), bf16), moved, edges, edges]
        + [quarters, quarters, quarter, quarter, vmem((m, n // m, share, LANES), f32)]
        + [lines, lines, vmem((8, LANES), f32), lines]
        + [vmem((tiles, 16, LANES), f32), vmem((tiles, n, 16, LANES), f32)]
        + [pltpu.SemaphoreType.DMA((8,)), pltpu.SemaphoreType.DMA((2, 13, n - 1))]
        + [pltpu.SemaphoreType.DMA((2, 3, m - 1))],
        compiler_params=pltpu.CompilerParams(
            collective_id=0, has_side_effects=True, vmem_limit_bytes=56 << 20
        ),
    )(
        proj_in, out_grad, long_filter, taps, swap_matrix(reps, LANES // reps), half_tables(tokens)
    )
    out, long_grad, tap_grad = pl.pallas_call(
        hand_over,
        out_shape=tuple(shape(x.shape, x.dtype) for x in (out, long_grad, tap_grad)),
        in_specs=[pl.BlockSpec(memory_space=pl.ANY)] * 3,
        out_specs=[pl.BlockSpec(memory_space=pl.ANY)] * 3,
        scratch_shapes=[vmem(x.shape, x.dtype) for x in (out, long_grad, tap_grad)]
        + [pltpu.SemaphoreType.DMA((2, streams + 2))],
    )(out, long_grad, tap_grad)
    return (out, long_grad.T, tap_grad)


def fits(n, m, proj_in, taps, long_filter, out_grad):
    streams, rows, channels = proj_in.shape
    groups = long_filter.shape[1]
    if channels % groups or groups % n or n % m or streams != 3 or taps.shape[1] != 3:
        return False
    reps, width = channels // groups, groups // n
    if reps < 2 or reps * width != LANES or n % reps or rows % (8 * reps * m) or rows % LANES:
        return False
    if n % 8 or reps * 3 > 16 or n // 2 % reps:
        return False
    return n * rows <= TABLE_LIMIT and n * rows % 1024 == 0


def routed(n, m, *arrays):
    return fast_shards(n, m, *arrays) if fits(n, m, *arrays) else shards(*arrays)


def solution(mesh):
    return jax.shard_map(
        functools.partial(routed, mesh.shape["seq"], mesh.shape["chan"]),
        mesh=mesh,
        in_specs=(P(None, "seq", "chan"), P(None, None, "chan"), P("seq", None), P("seq", "chan")),
        out_specs=(P(None, "seq", "chan"), P("seq", "chan"), P(None, None, "chan")),
        check_vma=False,
    )
```

```python
import functools
import math

import jax
import jax.numpy as jnp
import numpy as np
from jax import lax
from jax.experimental import pallas as pl
from jax.experimental.pallas import tpu as pltpu
from jax.sharding import PartitionSpec as P

MESH = pl.DeviceIdType.MESH
LANES = 128
TABLE_LIMIT = 1024
LEVELS = 250.0
RIM = 2
TABLES = 12


def shifted(x, axis, by):
    devices = lax.axis_size(axis)
    pairs = [(i, i + by) for i in range(devices) if 0 <= i + by < devices]
    return lax.ppermute(x, axis, pairs)


def angle_table(left_index, right_index, period):
    product = left_index[:, None] * right_index[None, :] % period
    phase = product.astype(jnp.float32) * (2.0 * math.pi / period)
    return (jnp.cos(phase), jnp.sin(phase))


def contract(pattern, factor_table, operand):
    return jnp.einsum(pattern, factor_table, operand, precision=lax.Precision.HIGHEST)


def steps_of(count):
    return jnp.arange(count, dtype=jnp.int32)


def whole_forward(signal, seq_width):
    tok_rows, stack_count, channels = signal.shape
    period = 2 * seq_width * tok_rows
    narrow = channels // seq_width
    arrived = lax.all_to_all(signal, "seq", split_axis=2, concat_axis=0, tiled=True)
    laid = arrived.reshape(seq_width, tok_rows, stack_count, narrow).transpose(2, 3, 0, 1)
    cos_step, sin_step = angle_table(steps_of(2 * seq_width), steps_of(seq_width), 2 * seq_width)
    real_part = contract("qm,ncmj->ncqj", cos_step, laid)
    imag_part = -contract("qm,ncmj->ncqj", sin_step, laid)
    cos_turn, sin_turn = angle_table(steps_of(2 * seq_width), steps_of(tok_rows), period)
    turned_re = real_part * cos_turn + imag_part * sin_turn
    turned_im = imag_part * cos_turn - real_part * sin_turn
    cos_row, sin_row = angle_table(steps_of(tok_rows), steps_of(tok_rows), tok_rows)
    spec_re = contract("rj,ncqj->ncqr", cos_row, turned_re) + contract(
        "rj,ncqj->ncqr", sin_row, turned_im
    )
    spec_im = contract("rj,ncqj->ncqr", cos_row, turned_im) - contract(
        "rj,ncqj->ncqr", sin_row, turned_re
    )
    return (spec_re, spec_im)


def whole_inverse(spec_re, spec_im, seq_width):
    stack_count, narrow, freq_count, tok_rows = spec_re.shape
    period = 2 * seq_width * tok_rows
    cos_row, sin_row = angle_table(steps_of(tok_rows), steps_of(tok_rows), tok_rows)
    back_re = contract("rj,ncqr->ncqj", cos_row, spec_re) - contract(
        "rj,ncqr->ncqj", sin_row, spec_im
    )
    back_im = contract("rj,ncqr->ncqj", sin_row, spec_re) + contract(
        "rj,ncqr->ncqj", cos_row, spec_im
    )
    cos_turn, sin_turn = angle_table(steps_of(freq_count), steps_of(tok_rows), period)
    turned_re = back_re * cos_turn - back_im * sin_turn
    turned_im = back_re * sin_turn + back_im * cos_turn
    cos_step, sin_step = angle_table(steps_of(seq_width), steps_of(freq_count), freq_count)
    signal = contract("mq,ncqj->ncmj", cos_step, turned_re) - contract(
        "mq,ncqj->ncmj", sin_step, turned_im
    )
    signal = (
        (signal / period).transpose(2, 3, 0, 1).reshape(seq_width * tok_rows, stack_count, narrow)
    )
    return lax.all_to_all(signal, "seq", split_axis=0, concat_axis=2, tiled=True)


def member(values, index, stack_axis):
    return lax.index_in_dim(values, index, stack_axis, keepdims=False)


def shards(proj_in, taps, long_filter, out_grad):
    stream_count, tok_rows, channels = proj_in.shape
    tap_count = taps.shape[1]
    groups = long_filter.shape[1]
    seq_width = lax.axis_size("seq")
    lower_rim = shifted(proj_in[:, tok_rows - (tap_count - 1) :, :], "seq", 1)
    extended = jnp.concatenate([lower_rim, proj_in], axis=1).astype(jnp.float32)
    lagged = [
        extended[:, tap_count - 1 - lag_step : tap_count - 1 - lag_step + tok_rows, :]
        for lag_step in range(tap_count)
    ]
    featured = taps[:, 0, None, :] * lagged[0]
    for lag_step in range(1, tap_count):
        featured = featured + taps[:, lag_step, None, :] * lagged[lag_step]
    query_rows, key_rows, value_rows = (featured[0], featured[1], featured[2])
    mixed_rows = key_rows * value_rows
    upstream = out_grad.astype(jnp.float32)
    conv_grad = upstream * query_rows
    tiled_filter = jnp.tile(long_filter, (1, channels // groups))
    signals = jnp.stack([mixed_rows, conv_grad, tiled_filter], axis=1)
    data_re, data_im = whole_forward(signals, seq_width)
    stack_axis = 0
    mix_re, mix_im = (member(data_re, 0, stack_axis), member(data_im, 0, stack_axis))
    grad_re, grad_im = (member(data_re, 1, stack_axis), member(data_im, 1, stack_axis))
    filt_re, filt_im = (member(data_re, 2, stack_axis), member(data_im, 2, stack_axis))
    conv_re = filt_re * mix_re - filt_im * mix_im
    conv_im = filt_re * mix_im + filt_im * mix_re
    back_re = filt_re * grad_re + filt_im * grad_im
    back_im = filt_re * grad_im - filt_im * grad_re
    corr_re = grad_re * mix_re + grad_im * mix_im
    corr_im = grad_im * mix_re - grad_re * mix_im
    prod_re = jnp.stack([conv_re, back_re, corr_re], axis=stack_axis)
    prod_im = jnp.stack([conv_im, back_im, corr_im], axis=stack_axis)
    outputs = whole_inverse(prod_re, prod_im, seq_width)
    conv_out, mixed_grad = (outputs[:, 0], outputs[:, 1])
    filt_grad = jnp.sum(outputs[:, 2].reshape(tok_rows, channels // groups, groups), axis=1)
    long_grad = lax.psum_scatter(filt_grad, "chan", scatter_dimension=1, tiled=True)
    feature_grad = jnp.stack(
        [upstream * conv_out, mixed_grad * value_rows, mixed_grad * key_rows], axis=0
    )
    upper_rim = shifted(feature_grad[:, : tap_count - 1, :], "seq", -1)
    trailing = jnp.concatenate([feature_grad, upper_rim], axis=1)
    input_grad = taps[:, 0, None, :] * feature_grad
    for lag_step in range(1, tap_count):
        input_grad = (
            input_grad + taps[:, lag_step, None, :] * trailing[:, lag_step : lag_step + tok_rows]
        )
    partial_taps = jnp.stack(
        [jnp.sum(feature_grad * lagged[lag_step], axis=1) for lag_step in range(tap_count)], axis=1
    )
    tap_grad = lax.psum(partial_taps, "seq") / math.sqrt(seq_width * tok_rows)
    return (input_grad.astype(jnp.bfloat16), long_grad, tap_grad)


def greet(axis_sizes):
    barrier = pltpu.get_barrier_semaphore()
    for axis, size in axis_sizes:
        me = lax.axis_index(axis)
        for j in range(1, size):
            pl.semaphore_signal(
                barrier, inc=1, device_id={axis: lax.rem(me + j, size)}, device_id_type=MESH
            )


def welcome(sizes):
    pl.semaphore_wait(pltpu.get_barrier_semaphore(), sum(size - 1 for size in sizes))


def swap_matrix(reps, width):
    side = reps * LANES
    row, col = np.arange(side)[:, None], np.arange(side)[None, :]
    outer, inner, rest = row // LANES, (row % LANES) // width, row % width
    return (inner * LANES + outer * width + rest == col).astype(jnp.bfloat16)


def lane_group(rows, width):
    return lax.broadcasted_iota(jnp.int32, (rows, LANES), 1) // width


def row_of(shape):
    return lax.broadcasted_iota(jnp.int32, shape, 0)


def turn(x, shift, axis):
    shift = shift % x.shape[axis]
    return x if shift == 0 else pltpu.roll(x, shift, axis)


def halves(x):
    high = x.astype(jnp.bfloat16)
    return high, (x - high.astype(jnp.float32)).astype(jnp.bfloat16)


def later(x):
    return jnp.where(row_of(x.shape) < 1, 0.0, pltpu.roll(x, 1, 0))


def sooner(x):
    rows = x.shape[0]
    return jnp.where(row_of(x.shape) >= rows - 1, 0.0, pltpu.roll(x, rows - 1, 0))


def group_sum(x, reps):
    step = LANES // reps
    if reps & (reps - 1):
        return sum((turn(x, r * step, 1) for r in range(1, reps)), x)
    while step < LANES:
        x = x + turn(x, step, 1)
        step *= 2
    return x


def scale_of(size):
    top = jnp.max(size, axis=0, keepdims=True)
    return jnp.maximum(top * (1.0 + 2.0**-7), 1e-30).astype(jnp.bfloat16).astype(jnp.float32)


def code_of(x, size, scale):
    level = jnp.exp2(size * (LEVELS / scale) - 0.5 * LEVELS)
    return jnp.where(x < 0.0, -level, level)


def encode(x):
    size = jnp.abs(x)
    first = jnp.where(row_of((8, LANES)) < RIM, 0.0, size[:8])
    scale = scale_of(jnp.concatenate([first, size[8:]], axis=0))
    level = code_of(x, size, scale)
    first = jnp.where(row_of((8, LANES)) < RIM, scale, level[:8])
    return jnp.concatenate([first, level[8:]], axis=0).astype(jnp.bfloat16)


def decode(code, scale=None):
    scale = code[:1] if scale is None else scale
    size = (jnp.log(jnp.abs(code)) * (1.0 / (math.log(2.0) * LEVELS)) + 0.5) * scale
    return jnp.where(code < 0.0, -size, size)


def dot(left, right):
    return jnp.dot(left, right, preferred_element_type=jnp.float32)


def three(high, low, x_high, x_low):
    return dot(high, x_high) + (dot(high, x_low) + dot(low, x_high))


def paired(high, low, both):
    wide = dot(high, both)
    return wide[:, :LANES] + (wide[:, LANES:] + dot(low, both[:, :LANES]))


def alternating(count):
    return jnp.where(row_of((count, LANES)) % 2 == 0, 1.0, -1.0)


def whole_kernel(
    n, m, reps, x_hbm, og_hbm, lf_hbm, tp_hbm, tb_hbm, out_ref, lo_ref, to_ref,
    x_ref, og_ref, lf_ref, tp_ref, tb, ex, es, er, exf, xs, xr, kf, vf, fs, fr, buf, both_e, both_o, fsp, gsp, pq_e, pq_o, eh, el, oh, ol,
    half_out, corr, codes, igr, back, backr, lgs, lgc, lsum, lgr, l2, ts, tc, tg, us, uc, ug, lsem, sems, csems,
):
    me, mine = lax.axis_index("seq"), lax.axis_index("chan")
    width = LANES // reps
    streams, rows, _ = x_ref.shape
    tap_count = tp_ref.shape[1]
    tokens = n * rows
    half = tokens // 2
    near = n // 2
    part = rows // reps
    share = part // m
    tiles = n // reps
    f32, bf16 = jnp.float32, jnp.bfloat16
    pairs = [
        (lf_hbm, lf_ref), (og_hbm, og_ref), (x_hbm.at[0], x_ref.at[0]), (tp_hbm, tp_ref),
        (tb_hbm.at[TABLES], tb.at[TABLES]), (x_hbm.at[1], x_ref.at[1]), (x_hbm.at[2], x_ref.at[2]),
        (tb_hbm.at[:TABLES], tb.at[:TABLES]),
    ]
    fetched = [pltpu.make_async_copy(*pair, lsem.at[i]) for i, pair in enumerate(pairs)]
    for copy in fetched:
        copy.start()
    sw_ref = tb.at[TABLES]
    grp = lane_group(part, width)
    greet([("seq", n), ("chan", m)])
    fetched[0].wait()
    scales = []

    def remote(kind, slot, source, target, peer):
        copy = pltpu.make_async_remote_copy(
            src_ref=source, dst_ref=target, send_sem=sems.at[0, kind, slot],
            recv_sem=sems.at[1, kind, slot], device_id={"seq": peer}, device_id_type=MESH,
        )
        copy.start()
        return copy

    def ship(kind, source, target):
        return [
            remote(kind, j - 1, source(lax.rem(me + j, n)), target, lax.rem(me + j, n))
            for j in sorted(range(1, n), key=lambda j: abs(2 * j - n))
        ]

    def spread(kind, source, target):
        copies = []
        for j in range(1, m):
            peer = lax.rem(mine + j, m)
            copy = pltpu.make_async_remote_copy(
                src_ref=source(peer), dst_ref=target, send_sem=csems.at[0, kind, j - 1],
                recv_sem=csems.at[1, kind, j - 1], device_id={"chan": peer}, device_id_type=MESH,
            )
            copy.start()
            copies.append(copy)
        return copies

    def place(r, h):
        return pl.ds(pl.multiple_of((r * tiles + h) * LANES, LANES), LANES)

    def feature(p, at):
        x = x_ref[p, :, at].astype(f32)
        total = tp_ref[p, 0:1, at] * x
        for lag in range(1, tap_count):
            total = total + tp_ref[p, lag : lag + 1, at] * pltpu.roll(x, lag, 0)
        return total

    def send_layout(pieces, place_at):
        moved = dot(jnp.concatenate(pieces, axis=1), sw_ref[...]).astype(bf16)
        for g in range(reps):
            place_at(g)[...] = moved[:, g * LANES : (g + 1) * LANES]

    for s in range(n):
        base = (s // reps) * LANES
        packed = jnp.zeros((part, LANES), f32)
        for q in range(reps):
            tile = lf_ref[q * part : (q + 1) * part, base : base + LANES]
            packed = jnp.where(grp == q, turn(tile, (q - s % reps) * width, 1), packed)
        size = jnp.abs(packed)
        scales.append(scale_of(size))
        fs[s] = code_of(packed, size, scales[s]).astype(bf16)
    for copy in fetched[1:-1]:
        copy.wait()
    welcome([n, m])
    filter_sent = ship(0, lambda peer: fs.at[peer], fr.at[me])
    fr[me] = fs[me]
    ex[...] = jnp.zeros_like(ex)
    for p in range(streams):
        ex[RIM * p : RIM * (p + 1), :] = x_ref[p, :16, :].astype(f32)[:RIM]
        ex[8 + RIM * p : 8 + RIM * (p + 1), :] = x_ref[p, rows - 16 :, :].astype(f32)[16 - RIM :]
    ex[RIM * streams : RIM * (streams + 1), :] = og_ref[:16, :].astype(f32)[:RIM]
    for h in range(tiles):
        joined = jnp.concatenate([ex[:, place(r, h)].astype(bf16) for r in range(reps)], axis=1)
        moved = dot(joined, sw_ref[...])
        for g in range(reps):
            block = moved[:, g * LANES : (g + 1) * LANES]
            block = jnp.where(row_of((16, LANES)) == 14, scales[h * reps + g], block)
            es[h * reps + g] = block.astype(bf16)
    rims_sent = ship(1, lambda peer: es.at[peer], er.at[me])
    side = me // near

    def halves_of_ship(kind, plane, piece):
        copies = []
        for step in range(2):
            which = (1 - side) if step == 0 else side
            for k in range(near // reps):
                h = which * (near // reps) + k
                send_layout([piece(place(r, h)) for r in range(reps)], lambda g: xs.at[plane, h * reps + g])
            for i in range(step, near):
                peer = which * near + lax.rem(me + i, near)
                copies.append(
                    remote(kind, step * near + i - step, xs.at[plane, peer], xr.at[plane, me], peer)
                )
        return copies

    def mixed_piece(at):
        key, value = feature(1, at), feature(2, at)
        kf[:, at], vf[:, at] = key, value
        return encode(key * value)

    first = halves_of_ship(2, 0, lambda at: encode(og_ref[:, at].astype(f32) * feature(0, at)))
    second = halves_of_ship(3, 1, mixed_piece)
    er[me] = es[me]
    xr[0, me] = xs[0, me]
    xr[1, me] = xs[1, me]

    taps = []
    home, slot = me // reps, lax.rem(me, reps)
    for p in range(streams):
        mixed_taps = jnp.zeros((tap_count, LANES), f32)
        for r in range(reps):
            at = pl.multiple_of((r * tiles + home) * LANES, LANES)
            tile = tp_ref[p, :, pl.ds(at, LANES)]
            shift = lax.rem((r + reps - slot) * width, LANES)
            mixed_taps = jnp.where(
                lane_group(tap_count, width) == r, pltpu.roll(tile, shift, 1), mixed_taps
            )
        taps.append([mixed_taps[i : i + 1] for i in range(tap_count)])

    def split():
        ends = []
        for part_of, both in ((0, both_e), (1, both_o)):
            values = buf[pl.ds(part_of, half, stride=2), :]
            both[:, :LANES], both[:, LANES:] = halves(values)
            ends.append(jnp.sum(alternating(half) * values, axis=0, keepdims=True))
        return ends

    chunk = min(256, half)

    def spectra(at):
        return [
            paired(tb[2 * table + 0, at, :], tb[2 * table + 1, at, :], both[...])
            for table, both in ((0, both_e), (1, both_e), (2, both_o), (3, both_o))
        ]

    def store_products(at, low, even_cos, even_sin, odd_cos, odd_sin):
        pq_e[at, :LANES], pq_e[at, LANES:] = halves(even_cos)
        pq_e[low, :LANES], pq_e[low, LANES:] = halves(even_sin)
        pq_o[at, :LANES], pq_o[at, LANES:] = halves(odd_cos)
        pq_o[low, :LANES], pq_o[low, LANES:] = halves(odd_sin)

    def inverse(at, end_e, end_o):
        even = paired(tb[0, at, :], tb[1, at, :], pq_e[:half])
        even = even + paired(tb[2, at, :], tb[3, at, :], pq_e[half:])
        odd = paired(tb[8, at, :], tb[9, at, :], pq_o[:half])
        odd = odd + paired(tb[10, at, :], tb[11, at, :], pq_o[half:])
        sign = alternating(chunk)
        return [even + sign * end_e], [odd + sign * end_o]

    def inverse_both(at, end_e, end_o):
        even = three(tb[0, at, :], tb[1, at, :], eh[:half], el[:half])
        even = even + three(tb[2, at, :], tb[3, at, :], eh[half:], el[half:])
        odd = three(tb[8, at, :], tb[9, at, :], oh[:half], ol[:half])
        odd = odd + three(tb[10, at, :], tb[11, at, :], oh[half:], ol[half:])
        sign = alternating(chunk)
        lanes = (slice(0, LANES), slice(LANES, 2 * LANES))
        return tuple(
            [value[:, lane] + sign * end[k] for k, lane in enumerate(lanes)]
            for value, end in ((even, end_e), (odd, end_o))
        )

    def return_layout(kind, inverse_of, end_e, end_o, between=lambda: None):
        copies = []
        for step in range(2):
            which = (1 - side) if step == 0 else side
            for c in range(half // 2 // chunk):
                at = pl.ds(pl.multiple_of(which * (half // 2) + c * chunk, chunk), chunk)
                for offset, values in enumerate(inverse_of(at, end_e, end_o)):
                    for value, place_of in zip(values, (half_out, corr)):
                        place_of[step, pl.ds(2 * c * chunk + offset, chunk, stride=2), :] = value
            for i in range(near):
                codes[kind, step, i] = encode(half_out[step, i * rows : (i + 1) * rows, :])
            if step == 1:
                between()
            for i in range(step, near):
                inner = lax.rem(me + i, near)
                copies.append(
                    remote(
                        4 + 2 * kind, step * near + i - step, codes.at[kind, step, inner],
                        igr.at[kind, me], which * near + inner,
                    )
                )
        igr[kind, me] = codes[kind, 1, lax.rem(me, near)]
        rims = []
        for i in range(RIM):
            far_rows = half_out[0, pl.ds(i, near, stride=rows), :]
            near_rows = half_out[1, pl.ds(i, near, stride=rows), :]
            low = jnp.where(side == 0, near_rows, far_rows)
            high = jnp.where(side == 0, far_rows, near_rows)
            rims.append(jnp.concatenate([low, high], axis=0))
        return copies, rims

    def return_rims(kind, grads):
        if len(grads) == 1:
            back[kind, ...] = jnp.zeros_like(back[kind])
        for k, pair in enumerate(grads):
            for i in range(RIM):
                back[kind, pl.ds(RIM * k + i, n, stride=8), :] = pair[i]
                back[kind, pl.ds(RIM * (k + len(grads)) + i, n, stride=8), :] = sooner(pair[i])
        mine_at = pl.ds(pl.multiple_of(me * 8, 8), 8)
        backr[kind, mine_at, :] = back[kind, mine_at, :]
        return ship(
            5 + 2 * kind, lambda peer: back.at[kind, pl.ds(pl.multiple_of(peer * 8, 8), 8)],
            backr.at[kind, mine_at],
        )

    for copy in filter_sent + rims_sent:
        copy.wait()
    exf[...] = er[...].reshape(n * 16, LANES).astype(f32)

    def rim(i):
        return exf[pl.ds(i, n, stride=16), :]

    def rim_feature(p):
        now, before = [rim(RIM * p), rim(RIM * p + 1)], [rim(8 + RIM * p + 1), rim(8 + RIM * p)]
        near_rows = [now[1], now[0], later(before[0]), later(before[1])]
        out = []
        for i in range(RIM):
            total = taps[p][0] * near_rows[1 - i]
            for lag in range(1, tap_count):
                total = total + taps[p][lag] * near_rows[1 - i + lag]
            out.append(total)
        return out

    query_rim, key_rim, value_rim = (rim_feature(p) for p in range(streams))
    grad_rim = [rim(RIM * streams), rim(RIM * streams + 1)]

    def collect(k, rims):
        for s in range(n):
            buf[s * rows : (s + 1) * rows, :] = decode(xr[k, s].astype(f32))
        for i in range(RIM):
            buf[pl.ds(i, n, stride=rows), :] = rims[i]

    for s in range(n):
        packed = decode(fr[s].astype(f32), exf[16 * s + 14 : 16 * s + 15, :])
        for q in range(reps):
            at = s * rows + q * part
            buf[at : at + part, :] = group_sum(jnp.where(grp == q, packed, 0.0), reps)
    filt_e, filt_o = split()
    fetched[-1].wait()

    @pl.loop(0, half // chunk)
    def _(i):
        at = pl.ds(pl.multiple_of(i * chunk, chunk), chunk)
        weight = jnp.where(row_of((chunk, LANES)) + i * chunk == 0, 1.0 / tokens, 2.0 / tokens)
        for k, value in enumerate(spectra(at)):
            fsp[k, at, :] = value * weight

    for copy in first:
        copy.wait()
    collect(0, [grad_rim[i] * query_rim[i] for i in range(RIM)])
    grad_e, grad_o = split()

    @pl.loop(0, half // chunk)
    def _(i):
        at = pl.ds(pl.multiple_of(i * chunk, chunk), chunk)
        low = pl.ds(pl.multiple_of(half + i * chunk, chunk), chunk)
        ge, te, go, to = spectra(at)
        for k, value in enumerate((ge, te, go, to)):
            gsp[k, at, :] = value
        fe, se, fo, so = (fsp[k, at, :] for k in range(4))
        store_products(
            at, low,
            fe * ge + fo * go + se * te + so * to,
            fe * te + fo * to - se * ge - so * go,
            fe * go + fo * ge + se * to + so * te,
            fe * to + fo * te - se * go - so * ge,
        )

    back_sent, back_rim = return_layout(
        0, inverse, (filt_e * grad_e + filt_o * grad_o) * (1.0 / tokens),
        (filt_e * grad_o - filt_o * grad_e) * (1.0 / tokens),
    )
    back_rims_sent = return_rims(
        0, [[back_rim[i] * value_rim[i] for i in range(RIM)], [back_rim[i] * key_rim[i] for i in range(RIM)]]
    )

    for copy in second:
        copy.wait()
    collect(1, [key_rim[i] * value_rim[i] for i in range(RIM)])
    mixed_e, mixed_o = split()

    @pl.loop(0, half // chunk)
    def _(i):
        at = pl.ds(pl.multiple_of(i * chunk, chunk), chunk)
        low = pl.ds(pl.multiple_of(half + i * chunk, chunk), chunk)
        he, ye, ho, yo = spectra(at)
        fe, se, fo, so = (fsp[k, at, :] for k in range(4))
        ge, te, go, to = (gsp[k, at, :] for k in range(4))
        weight = jnp.where(row_of((chunk, LANES)) + i * chunk == 0, 1.0 / tokens, 2.0 / tokens)

        def put(high, low_part, rows_at, conv, cross):
            high[rows_at, :LANES], low_part[rows_at, :LANES] = halves(conv)
            high[rows_at, LANES:], low_part[rows_at, LANES:] = halves(cross * weight)

        put(
            eh, el, at, fe * he + fo * ho - se * ye - so * yo,
            ge * he + go * ho + te * ye + to * yo,
        )
        put(
            eh, el, low, fe * ye + fo * yo + se * he + so * ho,
            te * he + to * ho - ge * ye - go * yo,
        )
        put(
            oh, ol, at, fe * ho + fo * he - se * yo - so * ye,
            ge * ho + go * he + te * yo + to * ye,
        )
        put(
            oh, ol, low, fe * yo + fo * ye + se * ho + so * he,
            te * ho + to * he - ge * yo - go * ye,
        )

    long_parts = []

    def filter_terms():
        for s in range(n):
            packed = jnp.zeros((part, LANES), f32)
            for q in range(reps):
                at = s % near * rows + q * part
                step = jnp.where(side == s // near, 1, 0)
                packed = jnp.where(grp == q, group_sum(corr[step, at : at + part, :], reps), packed)
            for k in range(m):
                lgs[k, s] = packed[k * share : (k + 1) * share]
        long_parts.extend(spread(1, lambda peer: lgs.at[peer], lgc.at[mine]))
        lgc[mine] = lgs[mine]

    inv = 1.0 / tokens
    conv_sent, conv_rim = return_layout(
        1, inverse_both,
        ((filt_e * mixed_e - filt_o * mixed_o) * inv, (grad_e * mixed_e + grad_o * mixed_o) * inv),
        ((filt_e * mixed_o + filt_o * mixed_e) * inv, (grad_o * mixed_e - grad_e * mixed_o) * inv),
        filter_terms,
    )
    conv_rims_sent = return_rims(1, [[conv_rim[i] * grad_rim[i] for i in range(RIM)]])

    def own_rims(kind, h, r):
        line = jnp.zeros((8, LANES), f32)
        for g in range(reps):
            at = (h * reps + g) * 8
            moved = turn(backr[kind, at : at + 8, :], (g - r) * width, 1)
            line = jnp.where(lane_group(8, width) == g, moved, line)
        return line

    def own_codes(kind, h):
        return dot(jnp.concatenate([igr[kind, h * reps + g] for g in range(reps)], axis=1), sw_ref[...])

    def finish(p, at, grads, own, after):
        row8 = row_of((8, LANES))
        first_rows = jnp.where(row8 == 0, own[0:1], jnp.where(row8 == 1, own[1:2], grads[:8]))
        grads = jnp.concatenate([first_rows, grads[8:]], axis=0)
        one, two = pltpu.roll(grads, rows - 1, 0), pltpu.roll(grads, rows - 2, 0)
        last = jnp.where(row8 == 7, after[0:1], one[rows - 8 :])
        one = jnp.concatenate([one[: rows - 8], last], axis=0)
        last = jnp.where(row8 == 7, after[1:2], jnp.where(row8 == 6, after[0:1], two[rows - 8 :]))
        two = jnp.concatenate([two[: rows - 8], last], axis=0)
        x = x_ref[p, :, at].astype(f32)
        total, lines = None, []
        for lag, value in enumerate((grads, one, two)):
            term = tp_ref[p, lag : lag + 1, at] * value
            total = term if total is None else total + term
            lines.append(jnp.sum(x * value, axis=0, keepdims=True) * (1.0 / math.sqrt(tokens)))
        out_ref[p, :, at] = total.astype(bf16)
        return lines

    for copy in long_parts:
        copy.wait()
    lsum[...] = sum((lgc[k] for k in range(1, m)), lgc[0])
    long_sent = ship(9, lambda peer: lsum.at[peer], lgr.at[me])
    lgr[me] = lsum[me]
    for copy in back_sent:
        copy.wait()
    for copy in back_rims_sent:
        copy.wait()
    ts[...] = jnp.zeros_like(ts)
    for h in range(tiles):
        moved = own_codes(0, h)
        for r in range(reps):
            at = place(r, h)
            grads = decode(moved[:, r * LANES : (r + 1) * LANES])
            edge = own_rims(0, h, r)
            for p, other in ((1, vf), (2, kf)):
                k = RIM * (p - 1)
                lines = finish(
                    p, at, grads * other[:, at], edge[k : k + RIM], edge[k + 4 : k + 4 + RIM]
                )
                for lag in range(tap_count):
                    at_row = RIM + (r * tiles + h) * 2 * tap_count + tap_count * (p - 1) + lag
                    ts[at_row : at_row + 1, :] = lines[lag]
    tc[...] = encode(ts[...])
    taps_sent = ship(8, lambda peer: tc, tg.at[me])
    tg[me] = tc[...]
    per = n // m

    for copy in conv_sent:
        copy.wait()
    for copy in conv_rims_sent:
        copy.wait()
    us[...] = jnp.zeros_like(us)
    query_sent = []
    for h in range(tiles):
        moved = own_codes(1, h)
        for r in range(reps):
            at = place(r, h)
            grads = decode(moved[:, r * LANES : (r + 1) * LANES]) * og_ref[:, at].astype(f32)
            edge = own_rims(1, h, r)
            lines = finish(0, at, grads, edge[:RIM], edge[RIM : 2 * RIM])
            for lag in range(tap_count):
                at_row = RIM + tap_count * r + lag
                us[h, at_row : at_row + 1, :] = lines[lag]
        uc[h] = encode(us[h])
        query_sent.append(ship(10 + h, lambda peer: uc.at[h], ug.at[h, me]))
        ug[h, me] = uc[h]
    for copy in long_sent:
        copy.wait()
    chan_sent = spread(0, lambda peer: lgr.at[pl.ds(peer * per, per)], l2.at[mine])
    l2[mine] = lgr[pl.ds(mine * per, per)]
    for copy in taps_sent:
        copy.wait()
    ts[...] = sum((decode(tg[s].astype(f32)) for s in range(1, n)), decode(tg[0].astype(f32)))
    for t in range(n):
        for p in (1, 2):
            at = RIM + 2 * tap_count * t + tap_count * (p - 1)
            to_ref[p, :, t * LANES : (t + 1) * LANES] = ts[at : at + tap_count, :]
    for copy in chan_sent:
        copy.wait()
    sources = [jnp.concatenate([l2[q, k] for q in range(m)], axis=0) for k in range(per)]
    lines = []
    for q in range(reps):
        line = jnp.zeros((part, LANES), f32)
        for k in range(per):
            line = jnp.where(grp == k, turn(sources[k], (k - q) * width, 1), line)
        lines.append(line)
    lo_ref[...] = jnp.concatenate(lines, axis=0).T[: per * width]
    for h in range(tiles):
        for copy in query_sent[h]:
            copy.wait()
        us[h] = sum((decode(ug[h, s].astype(f32)) for s in range(1, n)), decode(ug[h, 0].astype(f32)))
        for r in range(reps):
            at = RIM + tap_count * r
            to_ref[0, :, place(r, h)] = us[h, at : at + tap_count, :]


def hand_over(out_from, long_from, tap_from, out_to, long_to, tap_to, out_at, long_at, tap_at, sem):
    steps = [(out_from.at[p], out_at.at[p], out_to.at[p]) for p in range(out_from.shape[0])]
    steps += [(tap_from, tap_at, tap_to), (long_from, long_at, long_to)]
    inward = [pltpu.make_async_copy(a, b, sem.at[0, i]) for i, (a, b, _) in enumerate(steps)]
    outward = [pltpu.make_async_copy(b, c, sem.at[1, i]) for i, (_, b, c) in enumerate(steps)]
    for copy in inward:
        copy.start()
    for first, then in zip(inward, outward):
        first.wait()
        then.start()
    for copy in outward:
        copy.wait()


def whole_specs(count):
    return [pl.BlockSpec(memory_space=pltpu.VMEM)] * count


def tables_of(tokens, swap):
    half = tokens // 2
    freq, step = np.arange(half)[:, None], np.arange(half)[None, :]
    even = freq * (2 * step) % (2 * tokens) * (math.pi / tokens)
    odd = freq * (2 * step + 1) % (2 * tokens) * (math.pi / tokens)
    tables = [np.cos(even), np.sin(even), np.cos(odd), np.sin(odd), np.cos(odd).T, np.sin(odd).T]
    out = []
    for table in tables:
        high = table.astype(np.float32).astype(jnp.bfloat16)
        low = (table - high.astype(np.float64)).astype(np.float32).astype(jnp.bfloat16)
        out += [high, low]
    return np.stack(out + [swap])


def fast_shards(n, m, proj_in, taps, long_filter, out_grad):
    streams, rows, channels = proj_in.shape
    groups = long_filter.shape[1]
    reps = channels // groups
    part = rows // reps
    tokens = n * rows
    half = tokens // 2
    tiles = n // reps
    f32, bf16 = jnp.float32, jnp.bfloat16
    shape, vmem = jax.ShapeDtypeStruct, pltpu.VMEM
    share = part // m
    quarters = vmem((m, n, share, LANES), f32)
    quarter = vmem((n, share, LANES), f32)
    moved = vmem((2, n, rows, LANES), bf16)
    rims = vmem((n, 16, LANES), bf16)
    features = vmem((rows, channels), f32)
    both = vmem((half, 2 * LANES), bf16)
    spectrum = vmem((4, half, LANES), f32)
    products = vmem((tokens, 2 * LANES), bf16)
    edges = vmem((2, n * 8, LANES), f32)
    packed = vmem((n, part, LANES), bf16)
    out, long_grad, tap_grad = pl.pallas_call(
        functools.partial(whole_kernel, n, m, reps),
        out_shape=(
            shape((streams, rows, channels), bf16), shape((groups // m, rows), f32), shape(taps.shape, f32),
        ),
        in_specs=[pl.BlockSpec(memory_space=pl.ANY)] * 5,
        out_specs=whole_specs(3),
        scratch_shapes=[vmem(proj_in.shape, bf16), vmem(out_grad.shape, bf16)]
        + [vmem(long_filter.shape, f32), vmem(taps.shape, f32)]
        + [vmem((TABLES + 1, half, half), bf16), vmem((16, channels), f32), rims, rims]
        + [vmem((n * 16, LANES), f32), moved, moved, features, features]
        + [packed, packed, vmem((tokens, LANES), f32), both, both]
        + [spectrum, spectrum] + [products] * 6 + [vmem((2, half, LANES), f32)] * 2
        + [vmem((2, 2, n // 2, rows, LANES), bf16), moved, edges, edges]
        + [quarters, quarters, quarter, quarter, vmem((m, n // m, share, LANES), f32)]
        + [vmem((64, LANES), f32), vmem((64, LANES), bf16), vmem((n, 64, LANES), bf16)]
        + [vmem((tiles, 16, LANES), f32), vmem((tiles, 16, LANES), bf16), vmem((tiles, n, 16, LANES), bf16)]
        + [pltpu.SemaphoreType.DMA((8,)), pltpu.SemaphoreType.DMA((2, 12, n - 1))]
        + [pltpu.SemaphoreType.DMA((2, 2, m - 1))],
        compiler_params=pltpu.CompilerParams(
            collective_id=0, has_side_effects=True, vmem_limit_bytes=56 << 20
        ),
    )(proj_in, out_grad, long_filter, taps, tables_of(tokens, swap_matrix(reps, LANES // reps)))
    out, long_grad, tap_grad = pl.pallas_call(
        hand_over,
        out_shape=tuple(shape(x.shape, x.dtype) for x in (out, long_grad, tap_grad)),
        in_specs=[pl.BlockSpec(memory_space=pl.ANY)] * 3,
        out_specs=[pl.BlockSpec(memory_space=pl.ANY)] * 3,
        scratch_shapes=[vmem(x.shape, x.dtype) for x in (out, long_grad, tap_grad)]
        + [pltpu.SemaphoreType.DMA((2, streams + 2))],
    )(out, long_grad, tap_grad)
    return (out, long_grad.T, tap_grad)


def fits(n, m, proj_in, taps, long_filter, out_grad):
    streams, rows, channels = proj_in.shape
    groups = long_filter.shape[1]
    if channels % groups or groups % n or n % m or streams != 3 or taps.shape[1] != 3:
        return False
    reps, width = channels // groups, groups // n
    if reps < 2 or reps * width != LANES or n % reps or rows % (8 * reps * m) or rows % LANES:
        return False
    if reps * LANES != n * rows // 2:
        return False
    if n % 8 or reps * 3 + RIM > 16 or 6 * n + RIM > 64 or rows // reps % 16 or n // 2 % reps:
        return False
    return n * rows <= TABLE_LIMIT and n * rows % 1024 == 0


def routed(n, m, *arrays):
    return fast_shards(n, m, *arrays) if fits(n, m, *arrays) else shards(*arrays)


def solution(mesh):
    return jax.shard_map(
        functools.partial(routed, mesh.shape["seq"], mesh.shape["chan"]),
        mesh=mesh,
        in_specs=(P(None, "seq", "chan"), P(None, None, "chan"), P("seq", None), P("seq", "chan")),
        out_specs=(P(None, "seq", "chan"), P("seq", "chan"), P(None, None, "chan")),
        check_vma=False,
    )
```

```python
import functools
import math

import jax
import jax.numpy as jnp
import numpy as np
from jax import lax
from jax.experimental import pallas as pl
from jax.experimental.pallas import tpu as pltpu
from jax.sharding import PartitionSpec as P

MESH = pl.DeviceIdType.MESH
LANES = 128
TABLE_LIMIT = 1024
LEVELS = 250.0
RIM = 2
TABLES = 12


def shifted(x, axis, by):
    devices = lax.axis_size(axis)
    pairs = [(i, i + by) for i in range(devices) if 0 <= i + by < devices]
    return lax.ppermute(x, axis, pairs)


def angle_table(left_index, right_index, period):
    product = left_index[:, None] * right_index[None, :] % period
    phase = product.astype(jnp.float32) * (2.0 * math.pi / period)
    return (jnp.cos(phase), jnp.sin(phase))


def contract(pattern, factor_table, operand):
    return jnp.einsum(pattern, factor_table, operand, precision=lax.Precision.HIGHEST)


def steps_of(count):
    return jnp.arange(count, dtype=jnp.int32)


def whole_forward(signal, seq_width):
    tok_rows, stack_count, channels = signal.shape
    period = 2 * seq_width * tok_rows
    narrow = channels // seq_width
    arrived = lax.all_to_all(signal, "seq", split_axis=2, concat_axis=0, tiled=True)
    laid = arrived.reshape(seq_width, tok_rows, stack_count, narrow).transpose(2, 3, 0, 1)
    cos_step, sin_step = angle_table(steps_of(2 * seq_width), steps_of(seq_width), 2 * seq_width)
    real_part = contract("qm,ncmj->ncqj", cos_step, laid)
    imag_part = -contract("qm,ncmj->ncqj", sin_step, laid)
    cos_turn, sin_turn = angle_table(steps_of(2 * seq_width), steps_of(tok_rows), period)
    turned_re = real_part * cos_turn + imag_part * sin_turn
    turned_im = imag_part * cos_turn - real_part * sin_turn
    cos_row, sin_row = angle_table(steps_of(tok_rows), steps_of(tok_rows), tok_rows)
    spec_re = contract("rj,ncqj->ncqr", cos_row, turned_re) + contract(
        "rj,ncqj->ncqr", sin_row, turned_im
    )
    spec_im = contract("rj,ncqj->ncqr", cos_row, turned_im) - contract(
        "rj,ncqj->ncqr", sin_row, turned_re
    )
    return (spec_re, spec_im)


def whole_inverse(spec_re, spec_im, seq_width):
    stack_count, narrow, freq_count, tok_rows = spec_re.shape
    period = 2 * seq_width * tok_rows
    cos_row, sin_row = angle_table(steps_of(tok_rows), steps_of(tok_rows), tok_rows)
    back_re = contract("rj,ncqr->ncqj", cos_row, spec_re) - contract(
        "rj,ncqr->ncqj", sin_row, spec_im
    )
    back_im = contract("rj,ncqr->ncqj", sin_row, spec_re) + contract(
        "rj,ncqr->ncqj", cos_row, spec_im
    )
    cos_turn, sin_turn = angle_table(steps_of(freq_count), steps_of(tok_rows), period)
    turned_re = back_re * cos_turn - back_im * sin_turn
    turned_im = back_re * sin_turn + back_im * cos_turn
    cos_step, sin_step = angle_table(steps_of(seq_width), steps_of(freq_count), freq_count)
    signal = contract("mq,ncqj->ncmj", cos_step, turned_re) - contract(
        "mq,ncqj->ncmj", sin_step, turned_im
    )
    signal = (
        (signal / period).transpose(2, 3, 0, 1).reshape(seq_width * tok_rows, stack_count, narrow)
    )
    return lax.all_to_all(signal, "seq", split_axis=0, concat_axis=2, tiled=True)


def member(values, index, stack_axis):
    return lax.index_in_dim(values, index, stack_axis, keepdims=False)


def shards(proj_in, taps, long_filter, out_grad):
    stream_count, tok_rows, channels = proj_in.shape
    tap_count = taps.shape[1]
    groups = long_filter.shape[1]
    seq_width = lax.axis_size("seq")
    lower_rim = shifted(proj_in[:, tok_rows - (tap_count - 1) :, :], "seq", 1)
    extended = jnp.concatenate([lower_rim, proj_in], axis=1).astype(jnp.float32)
    lagged = [
        extended[:, tap_count - 1 - lag_step : tap_count - 1 - lag_step + tok_rows, :]
        for lag_step in range(tap_count)
    ]
    featured = taps[:, 0, None, :] * lagged[0]
    for lag_step in range(1, tap_count):
        featured = featured + taps[:, lag_step, None, :] * lagged[lag_step]
    query_rows, key_rows, value_rows = (featured[0], featured[1], featured[2])
    mixed_rows = key_rows * value_rows
    upstream = out_grad.astype(jnp.float32)
    conv_grad = upstream * query_rows
    tiled_filter = jnp.tile(long_filter, (1, channels // groups))
    signals = jnp.stack([mixed_rows, conv_grad, tiled_filter], axis=1)
    data_re, data_im = whole_forward(signals, seq_width)
    stack_axis = 0
    mix_re, mix_im = (member(data_re, 0, stack_axis), member(data_im, 0, stack_axis))
    grad_re, grad_im = (member(data_re, 1, stack_axis), member(data_im, 1, stack_axis))
    filt_re, filt_im = (member(data_re, 2, stack_axis), member(data_im, 2, stack_axis))
    conv_re = filt_re * mix_re - filt_im * mix_im
    conv_im = filt_re * mix_im + filt_im * mix_re
    back_re = filt_re * grad_re + filt_im * grad_im
    back_im = filt_re * grad_im - filt_im * grad_re
    corr_re = grad_re * mix_re + grad_im * mix_im
    corr_im = grad_im * mix_re - grad_re * mix_im
    prod_re = jnp.stack([conv_re, back_re, corr_re], axis=stack_axis)
    prod_im = jnp.stack([conv_im, back_im, corr_im], axis=stack_axis)
    outputs = whole_inverse(prod_re, prod_im, seq_width)
    conv_out, mixed_grad = (outputs[:, 0], outputs[:, 1])
    filt_grad = jnp.sum(outputs[:, 2].reshape(tok_rows, channels // groups, groups), axis=1)
    long_grad = lax.psum_scatter(filt_grad, "chan", scatter_dimension=1, tiled=True)
    feature_grad = jnp.stack(
        [upstream * conv_out, mixed_grad * value_rows, mixed_grad * key_rows], axis=0
    )
    upper_rim = shifted(feature_grad[:, : tap_count - 1, :], "seq", -1)
    trailing = jnp.concatenate([feature_grad, upper_rim], axis=1)
    input_grad = taps[:, 0, None, :] * feature_grad
    for lag_step in range(1, tap_count):
        input_grad = (
            input_grad + taps[:, lag_step, None, :] * trailing[:, lag_step : lag_step + tok_rows]
        )
    partial_taps = jnp.stack(
        [jnp.sum(feature_grad * lagged[lag_step], axis=1) for lag_step in range(tap_count)], axis=1
    )
    tap_grad = lax.psum(partial_taps, "seq") / math.sqrt(seq_width * tok_rows)
    return (input_grad.astype(jnp.bfloat16), long_grad, tap_grad)


def greet(axis_sizes):
    barrier = pltpu.get_barrier_semaphore()
    for axis, size in axis_sizes:
        me = lax.axis_index(axis)
        for j in range(1, size):
            pl.semaphore_signal(
                barrier, inc=1, device_id={axis: lax.rem(me + j, size)}, device_id_type=MESH
            )


def welcome(sizes):
    pl.semaphore_wait(pltpu.get_barrier_semaphore(), sum(size - 1 for size in sizes))


def swap_matrix(reps, width):
    side = reps * LANES
    row, col = np.arange(side)[:, None], np.arange(side)[None, :]
    outer, inner, rest = row // LANES, (row % LANES) // width, row % width
    return (inner * LANES + outer * width + rest == col).astype(jnp.bfloat16)


def lane_group(rows, width):
    return lax.broadcasted_iota(jnp.int32, (rows, LANES), 1) // width


def row_of(shape):
    return lax.broadcasted_iota(jnp.int32, shape, 0)


def turn(x, shift, axis):
    shift = shift % x.shape[axis]
    return x if shift == 0 else pltpu.roll(x, shift, axis)


def halves(x):
    high = x.astype(jnp.bfloat16)
    return high, (x - high.astype(jnp.float32)).astype(jnp.bfloat16)


def later(x):
    return jnp.where(row_of(x.shape) < 1, 0.0, pltpu.roll(x, 1, 0))


def sooner(x):
    rows = x.shape[0]
    return jnp.where(row_of(x.shape) >= rows - 1, 0.0, pltpu.roll(x, rows - 1, 0))


def group_sum(x, reps):
    step = LANES // reps
    if reps & (reps - 1):
        return sum((turn(x, r * step, 1) for r in range(1, reps)), x)
    while step < LANES:
        x = x + turn(x, step, 1)
        step *= 2
    return x


def scale_of(size):
    top = jnp.max(size, axis=0, keepdims=True)
    return jnp.maximum(top * (1.0 + 2.0**-7), 1e-30).astype(jnp.bfloat16).astype(jnp.float32)


def code_of(x, size, scale):
    level = jnp.exp2(size * (LEVELS / scale) - 0.5 * LEVELS)
    return jnp.where(x < 0.0, -level, level)


def encode(x):
    size = jnp.abs(x)
    first = jnp.where(row_of((8, LANES)) < RIM, 0.0, size[:8])
    scale = scale_of(jnp.concatenate([first, size[8:]], axis=0))
    level = code_of(x, size, scale)
    first = jnp.where(row_of((8, LANES)) < RIM, scale, level[:8])
    return jnp.concatenate([first, level[8:]], axis=0).astype(jnp.bfloat16)


def decode(code, scale=None):
    scale = code[:1] if scale is None else scale
    size = (jnp.log(jnp.abs(code)) * (1.0 / (math.log(2.0) * LEVELS)) + 0.5) * scale
    return jnp.where(code < 0.0, -size, size)


def dot(left, right):
    return jnp.dot(left, right, preferred_element_type=jnp.float32)


def three(high, low, x_high, x_low):
    return dot(high, x_high) + (dot(high, x_low) + dot(low, x_high))


def paired(high, low, both):
    wide = dot(high, both)
    return wide[:, :LANES] + (wide[:, LANES:] + dot(low, both[:, :LANES]))


def alternating(count):
    return jnp.where(row_of((count, LANES)) % 2 == 0, 1.0, -1.0)


def whole_kernel(
    n, m, reps, x_hbm, og_hbm, lf_hbm, tp_hbm, tb_hbm, out_ref, lo_ref, to_ref,
    x_ref, og_ref, lf_ref, tp_ref, tb, ex, es, er, exf, xs, xr, kf, vf, fs, fr, buf, both_e, both_o, fsp, gsp, pq_e, pq_o, eh, el, oh, ol,
    half_out, corr, codes, igr, back, backr, lgs, lgc, lsum, lgr, l2, ts, tc, tg, us, uc, ug, lsem, sems, csems,
):
    me, mine = lax.axis_index("seq"), lax.axis_index("chan")
    width = LANES // reps
    streams, rows, _ = x_ref.shape
    tap_count = tp_ref.shape[1]
    tokens = n * rows
    half = tokens // 2
    near = n // 2
    part = rows // reps
    share = part // m
    tiles = n // reps
    f32, bf16 = jnp.float32, jnp.bfloat16
    pairs = [
        (lf_hbm, lf_ref), (og_hbm, og_ref), (x_hbm.at[0], x_ref.at[0]), (tp_hbm, tp_ref),
        (tb_hbm.at[TABLES], tb.at[TABLES]), (x_hbm.at[1], x_ref.at[1]), (x_hbm.at[2], x_ref.at[2]),
        (tb_hbm.at[:TABLES], tb.at[:TABLES]),
    ]
    fetched = [pltpu.make_async_copy(*pair, lsem.at[i]) for i, pair in enumerate(pairs)]
    for copy in fetched:
        copy.start()
    sw_ref = tb.at[TABLES]
    grp = lane_group(part, width)
    greet([("seq", n), ("chan", m)])
    fetched[0].wait()
    scales = []

    def remote(kind, slot, source, target, peer):
        copy = pltpu.make_async_remote_copy(
            src_ref=source, dst_ref=target, send_sem=sems.at[0, kind, slot],
            recv_sem=sems.at[1, kind, slot], device_id={"seq": peer}, device_id_type=MESH,
        )
        copy.start()
        return copy

    def ship(kind, source, target):
        return [
            remote(kind, j - 1, source(lax.rem(me + j, n)), target, lax.rem(me + j, n))
            for j in sorted(range(1, n), key=lambda j: abs(2 * j - n))
        ]

    def spread(kind, source, target):
        copies = []
        for j in range(1, m):
            peer = lax.rem(mine + j, m)
            copy = pltpu.make_async_remote_copy(
                src_ref=source(peer), dst_ref=target, send_sem=csems.at[0, kind, j - 1],
                recv_sem=csems.at[1, kind, j - 1], device_id={"chan": peer}, device_id_type=MESH,
            )
            copy.start()
            copies.append(copy)
        return copies

    def place(r, h):
        return pl.ds(pl.multiple_of((r * tiles + h) * LANES, LANES), LANES)

    def feature(p, at):
        x = x_ref[p, :, at].astype(f32)
        total = tp_ref[p, 0:1, at] * x
        for lag in range(1, tap_count):
            total = total + tp_ref[p, lag : lag + 1, at] * pltpu.roll(x, lag, 0)
        return total

    def send_layout(pieces, place_at):
        moved = dot(jnp.concatenate(pieces, axis=1), sw_ref[...]).astype(bf16)
        for g in range(reps):
            place_at(g)[...] = moved[:, g * LANES : (g + 1) * LANES]

    for s in range(n):
        base = (s // reps) * LANES
        packed = jnp.zeros((part, LANES), f32)
        for q in range(reps):
            tile = lf_ref[q * part : (q + 1) * part, base : base + LANES]
            packed = jnp.where(grp == q, turn(tile, (q - s % reps) * width, 1), packed)
        size = jnp.abs(packed)
        scales.append(scale_of(size))
        fs[s] = code_of(packed, size, scales[s]).astype(bf16)
    for copy in fetched[1:-1]:
        copy.wait()
    ex[...] = jnp.zeros_like(ex)
    for p in range(streams):
        ex[RIM * p : RIM * (p + 1), :] = x_ref[p, :16, :].astype(f32)[:RIM]
        ex[8 + RIM * p : 8 + RIM * (p + 1), :] = x_ref[p, rows - 16 :, :].astype(f32)[16 - RIM :]
    ex[RIM * streams : RIM * (streams + 1), :] = og_ref[:16, :].astype(f32)[:RIM]
    for h in range(tiles):
        joined = jnp.concatenate([ex[:, place(r, h)].astype(bf16) for r in range(reps)], axis=1)
        moved = dot(joined, sw_ref[...])
        for g in range(reps):
            block = moved[:, g * LANES : (g + 1) * LANES]
            block = jnp.where(row_of((16, LANES)) == 14, scales[h * reps + g], block)
            es[h * reps + g] = block.astype(bf16)
    side = me // near

    def prepare(plane, piece, step):
        which = (1 - side) if step == 0 else side
        for k in range(near // reps):
            h = which * (near // reps) + k
            send_layout([piece(place(r, h)) for r in range(reps)], lambda g: xs.at[plane, h * reps + g])

    def send_half(kind, plane, step):
        which = (1 - side) if step == 0 else side
        copies = []
        for i in range(step, near):
            peer = which * near + lax.rem(me + i, near)
            copies.append(
                remote(kind, step * near + i - step, xs.at[plane, peer], xr.at[plane, me], peer)
            )
        return copies

    def mixed_piece(at):
        key, value = feature(1, at), feature(2, at)
        kf[:, at], vf[:, at] = key, value
        return encode(key * value)

    for step in range(2):
        prepare(0, lambda at: encode(og_ref[:, at].astype(f32) * feature(0, at)), step)
    welcome([n, m])
    filter_sent = ship(0, lambda peer: fs.at[peer], fr.at[me])
    rims_sent = ship(1, lambda peer: es.at[peer], er.at[me])
    first = send_half(2, 0, 0) + send_half(2, 0, 1)
    second = []
    for step in range(2):
        prepare(1, mixed_piece, step)
        second += send_half(3, 1, step)
    fr[me] = fs[me]
    er[me] = es[me]
    xr[0, me] = xs[0, me]
    xr[1, me] = xs[1, me]

    taps = []
    home, slot = me // reps, lax.rem(me, reps)
    for p in range(streams):
        mixed_taps = jnp.zeros((tap_count, LANES), f32)
        for r in range(reps):
            at = pl.multiple_of((r * tiles + home) * LANES, LANES)
            tile = tp_ref[p, :, pl.ds(at, LANES)]
            shift = lax.rem((r + reps - slot) * width, LANES)
            mixed_taps = jnp.where(
                lane_group(tap_count, width) == r, pltpu.roll(tile, shift, 1), mixed_taps
            )
        taps.append([mixed_taps[i : i + 1] for i in range(tap_count)])

    def split():
        ends = []
        for part_of, both in ((0, both_e), (1, both_o)):
            values = buf[pl.ds(part_of, half, stride=2), :]
            both[:, :LANES], both[:, LANES:] = halves(values)
            ends.append(jnp.sum(alternating(half) * values, axis=0, keepdims=True))
        return ends

    chunk = min(256, half)

    def spectra(at):
        return [
            paired(tb[2 * table + 0, at, :], tb[2 * table + 1, at, :], both[...])
            for table, both in ((0, both_e), (1, both_e), (2, both_o), (3, both_o))
        ]

    def store_products(at, low, even_cos, even_sin, odd_cos, odd_sin):
        pq_e[at, :LANES], pq_e[at, LANES:] = halves(even_cos)
        pq_e[low, :LANES], pq_e[low, LANES:] = halves(even_sin)
        pq_o[at, :LANES], pq_o[at, LANES:] = halves(odd_cos)
        pq_o[low, :LANES], pq_o[low, LANES:] = halves(odd_sin)

    def inverse(at, end_e, end_o):
        even = paired(tb[0, at, :], tb[1, at, :], pq_e[:half])
        even = even + paired(tb[2, at, :], tb[3, at, :], pq_e[half:])
        odd = paired(tb[8, at, :], tb[9, at, :], pq_o[:half])
        odd = odd + paired(tb[10, at, :], tb[11, at, :], pq_o[half:])
        sign = alternating(chunk)
        return [even + sign * end_e], [odd + sign * end_o]

    def inverse_both(at, end_e, end_o):
        even = three(tb[0, at, :], tb[1, at, :], eh[:half], el[:half])
        even = even + three(tb[2, at, :], tb[3, at, :], eh[half:], el[half:])
        odd = three(tb[8, at, :], tb[9, at, :], oh[:half], ol[:half])
        odd = odd + three(tb[10, at, :], tb[11, at, :], oh[half:], ol[half:])
        sign = alternating(chunk)
        lanes = (slice(0, LANES), slice(LANES, 2 * LANES))
        return tuple(
            [value[:, lane] + sign * end[k] for k, lane in enumerate(lanes)]
            for value, end in ((even, end_e), (odd, end_o))
        )

    def return_layout(kind, inverse_of, end_e, end_o, between=lambda: None):
        copies = []
        for step in range(2):
            which = (1 - side) if step == 0 else side
            for c in range(half // 2 // chunk):
                at = pl.ds(pl.multiple_of(which * (half // 2) + c * chunk, chunk), chunk)
                for offset, values in enumerate(inverse_of(at, end_e, end_o)):
                    for value, place_of in zip(values, (half_out, corr)):
                        place_of[step, pl.ds(2 * c * chunk + offset, chunk, stride=2), :] = value
            for i in range(near):
                codes[kind, step, i] = encode(half_out[step, i * rows : (i + 1) * rows, :])
            if step == 1:
                between()
            for i in range(step, near):
                inner = lax.rem(me + i, near)
                copies.append(
                    remote(
                        4 + 2 * kind, step * near + i - step, codes.at[kind, step, inner],
                        igr.at[kind, me], which * near + inner,
                    )
                )
        igr[kind, me] = codes[kind, 1, lax.rem(me, near)]
        rims = []
        for i in range(RIM):
            far_rows = half_out[0, pl.ds(i, near, stride=rows), :]
            near_rows = half_out[1, pl.ds(i, near, stride=rows), :]
            low = jnp.where(side == 0, near_rows, far_rows)
            high = jnp.where(side == 0, far_rows, near_rows)
            rims.append(jnp.concatenate([low, high], axis=0))
        return copies, rims

    def return_rims(kind, grads):
        if len(grads) == 1:
            back[kind, ...] = jnp.zeros_like(back[kind])
        for k, pair in enumerate(grads):
            for i in range(RIM):
                back[kind, pl.ds(RIM * k + i, n, stride=8), :] = pair[i]
                back[kind, pl.ds(RIM * (k + len(grads)) + i, n, stride=8), :] = sooner(pair[i])
        mine_at = pl.ds(pl.multiple_of(me * 8, 8), 8)
        backr[kind, mine_at, :] = back[kind, mine_at, :]
        return ship(
            5 + 2 * kind, lambda peer: back.at[kind, pl.ds(pl.multiple_of(peer * 8, 8), 8)],
            backr.at[kind, mine_at],
        )

    for copy in filter_sent + rims_sent:
        copy.wait()
    exf[...] = er[...].reshape(n * 16, LANES).astype(f32)

    def rim(i):
        return exf[pl.ds(i, n, stride=16), :]

    def rim_feature(p):
        now, before = [rim(RIM * p), rim(RIM * p + 1)], [rim(8 + RIM * p + 1), rim(8 + RIM * p)]
        near_rows = [now[1], now[0], later(before[0]), later(before[1])]
        out = []
        for i in range(RIM):
            total = taps[p][0] * near_rows[1 - i]
            for lag in range(1, tap_count):
                total = total + taps[p][lag] * near_rows[1 - i + lag]
            out.append(total)
        return out

    query_rim, key_rim, value_rim = (rim_feature(p) for p in range(streams))
    grad_rim = [rim(RIM * streams), rim(RIM * streams + 1)]

    def collect(k, rims):
        for s in range(n):
            buf[s * rows : (s + 1) * rows, :] = decode(xr[k, s].astype(f32))
        for i in range(RIM):
            buf[pl.ds(i, n, stride=rows), :] = rims[i]

    for s in range(n):
        packed = decode(fr[s].astype(f32), exf[16 * s + 14 : 16 * s + 15, :])
        for q in range(reps):
            at = s * rows + q * part
            buf[at : at + part, :] = group_sum(jnp.where(grp == q, packed, 0.0), reps)
    filt_e, filt_o = split()
    fetched[-1].wait()

    @pl.loop(0, half // chunk)
    def _(i):
        at = pl.ds(pl.multiple_of(i * chunk, chunk), chunk)
        weight = jnp.where(row_of((chunk, LANES)) + i * chunk == 0, 1.0 / tokens, 2.0 / tokens)
        for k, value in enumerate(spectra(at)):
            fsp[k, at, :] = value * weight

    for copy in first:
        copy.wait()
    collect(0, [grad_rim[i] * query_rim[i] for i in range(RIM)])
    grad_e, grad_o = split()

    @pl.loop(0, half // chunk)
    def _(i):
        at = pl.ds(pl.multiple_of(i * chunk, chunk), chunk)
        low = pl.ds(pl.multiple_of(half + i * chunk, chunk), chunk)
        ge, te, go, to = spectra(at)
        for k, value in enumerate((ge, te, go, to)):
            gsp[k, at, :] = value
        fe, se, fo, so = (fsp[k, at, :] for k in range(4))
        store_products(
            at, low,
            fe * ge + fo * go + se * te + so * to,
            fe * te + fo * to - se * ge - so * go,
            fe * go + fo * ge + se * to + so * te,
            fe * to + fo * te - se * go - so * ge,
        )

    back_sent, back_rim = return_layout(
        0, inverse, (filt_e * grad_e + filt_o * grad_o) * (1.0 / tokens),
        (filt_e * grad_o - filt_o * grad_e) * (1.0 / tokens),
    )
    back_rims_sent = return_rims(
        0, [[back_rim[i] * value_rim[i] for i in range(RIM)], [back_rim[i] * key_rim[i] for i in range(RIM)]]
    )

    for copy in second:
        copy.wait()
    collect(1, [key_rim[i] * value_rim[i] for i in range(RIM)])
    mixed_e, mixed_o = split()

    @pl.loop(0, half // chunk)
    def _(i):
        at = pl.ds(pl.multiple_of(i * chunk, chunk), chunk)
        low = pl.ds(pl.multiple_of(half + i * chunk, chunk), chunk)
        he, ye, ho, yo = spectra(at)
        fe, se, fo, so = (fsp[k, at, :] for k in range(4))
        ge, te, go, to = (gsp[k, at, :] for k in range(4))
        weight = jnp.where(row_of((chunk, LANES)) + i * chunk == 0, 1.0 / tokens, 2.0 / tokens)

        def put(high, low_part, rows_at, conv, cross):
            high[rows_at, :LANES], low_part[rows_at, :LANES] = halves(conv)
            high[rows_at, LANES:], low_part[rows_at, LANES:] = halves(cross * weight)

        put(
            eh, el, at, fe * he + fo * ho - se * ye - so * yo,
            ge * he + go * ho + te * ye + to * yo,
        )
        put(
            eh, el, low, fe * ye + fo * yo + se * he + so * ho,
            te * he + to * ho - ge * ye - go * yo,
        )
        put(
            oh, ol, at, fe * ho + fo * he - se * yo - so * ye,
            ge * ho + go * he + te * yo + to * ye,
        )
        put(
            oh, ol, low, fe * yo + fo * ye + se * ho + so * he,
            te * ho + to * he - ge * yo - go * ye,
        )

    long_parts = []

    def filter_terms():
        for s in range(n):
            packed = jnp.zeros((part, LANES), f32)
            for q in range(reps):
                at = s % near * rows + q * part
                step = jnp.where(side == s // near, 1, 0)
                packed = jnp.where(grp == q, group_sum(corr[step, at : at + part, :], reps), packed)
            for k in range(m):
                lgs[k, s] = packed[k * share : (k + 1) * share]
        long_parts.extend(spread(1, lambda peer: lgs.at[peer], lgc.at[mine]))
        lgc[mine] = lgs[mine]

    inv = 1.0 / tokens
    conv_sent, conv_rim = return_layout(
        1, inverse_both,
        ((filt_e * mixed_e - filt_o * mixed_o) * inv, (grad_e * mixed_e + grad_o * mixed_o) * inv),
        ((filt_e * mixed_o + filt_o * mixed_e) * inv, (grad_o * mixed_e - grad_e * mixed_o) * inv),
        filter_terms,
    )
    conv_rims_sent = return_rims(1, [[conv_rim[i] * grad_rim[i] for i in range(RIM)]])

    def own_rims(kind, h, r):
        line = jnp.zeros((8, LANES), f32)
        for g in range(reps):
            at = (h * reps + g) * 8
            moved = turn(backr[kind, at : at + 8, :], (g - r) * width, 1)
            line = jnp.where(lane_group(8, width) == g, moved, line)
        return line

    def own_codes(kind, h):
        return dot(jnp.concatenate([igr[kind, h * reps + g] for g in range(reps)], axis=1), sw_ref[...])

    def finish(p, at, grads, own, after):
        row8 = row_of((8, LANES))
        first_rows = jnp.where(row8 == 0, own[0:1], jnp.where(row8 == 1, own[1:2], grads[:8]))
        grads = jnp.concatenate([first_rows, grads[8:]], axis=0)
        one, two = pltpu.roll(grads, rows - 1, 0), pltpu.roll(grads, rows - 2, 0)
        last = jnp.where(row8 == 7, after[0:1], one[rows - 8 :])
        one = jnp.concatenate([one[: rows - 8], last], axis=0)
        last = jnp.where(row8 == 7, after[1:2], jnp.where(row8 == 6, after[0:1], two[rows - 8 :]))
        two = jnp.concatenate([two[: rows - 8], last], axis=0)
        x = x_ref[p, :, at].astype(f32)
        total, lines = None, []
        for lag, value in enumerate((grads, one, two)):
            term = tp_ref[p, lag : lag + 1, at] * value
            total = term if total is None else total + term
            lines.append(jnp.sum(x * value, axis=0, keepdims=True) * (1.0 / math.sqrt(tokens)))
        out_ref[p, :, at] = total.astype(bf16)
        return lines

    for copy in long_parts:
        copy.wait()
    lsum[...] = sum((lgc[k] for k in range(1, m)), lgc[0])
    long_sent = ship(9, lambda peer: lsum.at[peer], lgr.at[me])
    lgr[me] = lsum[me]
    for copy in back_sent:
        copy.wait()
    for copy in back_rims_sent:
        copy.wait()
    ts[...] = jnp.zeros_like(ts)
    for h in range(tiles):
        moved = own_codes(0, h)
        for r in range(reps):
            at = place(r, h)
            grads = decode(moved[:, r * LANES : (r + 1) * LANES])
            edge = own_rims(0, h, r)
            for p, other in ((1, vf), (2, kf)):
                k = RIM * (p - 1)
                lines = finish(
                    p, at, grads * other[:, at], edge[k : k + RIM], edge[k + 4 : k + 4 + RIM]
                )
                for lag in range(tap_count):
                    at_row = RIM + (r * tiles + h) * 2 * tap_count + tap_count * (p - 1) + lag
                    ts[at_row : at_row + 1, :] = lines[lag]
    tc[...] = encode(ts[...])
    taps_sent = ship(8, lambda peer: tc, tg.at[me])
    tg[me] = tc[...]
    per = n // m

    for copy in conv_sent:
        copy.wait()
    for copy in conv_rims_sent:
        copy.wait()
    us[...] = jnp.zeros_like(us)
    query_sent = []
    for h in range(tiles):
        moved = own_codes(1, h)
        for r in range(reps):
            at = place(r, h)
            grads = decode(moved[:, r * LANES : (r + 1) * LANES]) * og_ref[:, at].astype(f32)
            edge = own_rims(1, h, r)
            lines = finish(0, at, grads, edge[:RIM], edge[RIM : 2 * RIM])
            for lag in range(tap_count):
                at_row = RIM + tap_count * r + lag
                us[h, at_row : at_row + 1, :] = lines[lag]
        uc[h] = encode(us[h])
        query_sent.append(ship(10 + h, lambda peer: uc.at[h], ug.at[h, me]))
        ug[h, me] = uc[h]
    for copy in long_sent:
        copy.wait()
    chan_sent = spread(0, lambda peer: lgr.at[pl.ds(peer * per, per)], l2.at[mine])
    l2[mine] = lgr[pl.ds(mine * per, per)]
    for copy in taps_sent:
        copy.wait()
    ts[...] = sum((decode(tg[s].astype(f32)) for s in range(1, n)), decode(tg[0].astype(f32)))
    for t in range(n):
        for p in (1, 2):
            at = RIM + 2 * tap_count * t + tap_count * (p - 1)
            to_ref[p, :, t * LANES : (t + 1) * LANES] = ts[at : at + tap_count, :]
    for copy in chan_sent:
        copy.wait()
    sources = [jnp.concatenate([l2[q, k] for q in range(m)], axis=0) for k in range(per)]
    lines = []
    for q in range(reps):
        line = jnp.zeros((part, LANES), f32)
        for k in range(per):
            line = jnp.where(grp == k, turn(sources[k], (k - q) * width, 1), line)
        lines.append(line)
    lo_ref[...] = jnp.concatenate(lines, axis=0).T[: per * width]
    for h in range(tiles):
        for copy in query_sent[h]:
            copy.wait()
        us[h] = sum((decode(ug[h, s].astype(f32)) for s in range(1, n)), decode(ug[h, 0].astype(f32)))
        for r in range(reps):
            at = RIM + tap_count * r
            to_ref[0, :, place(r, h)] = us[h, at : at + tap_count, :]


def hand_over(out_from, long_from, tap_from, out_to, long_to, tap_to, sem):
    pairs = ((out_from, out_to), (tap_from, tap_to), (long_from, long_to))
    copies = [pltpu.make_async_copy(*pair, sem.at[i]) for i, pair in enumerate(pairs)]
    for copy in copies:
        copy.start()
    for copy in copies:
        copy.wait()


def whole_specs(count):
    return [pl.BlockSpec(memory_space=pltpu.VMEM)] * count


def tables_of(tokens, swap):
    half = tokens // 2
    freq, step = np.arange(half)[:, None], np.arange(half)[None, :]
    even = freq * (2 * step) % (2 * tokens) * (math.pi / tokens)
    odd = freq * (2 * step + 1) % (2 * tokens) * (math.pi / tokens)
    tables = [np.cos(even), np.sin(even), np.cos(odd), np.sin(odd), np.cos(odd).T, np.sin(odd).T]
    out = []
    for table in tables:
        high = table.astype(np.float32).astype(jnp.bfloat16)
        low = (table - high.astype(np.float64)).astype(np.float32).astype(jnp.bfloat16)
        out += [high, low]
    return np.stack(out + [swap])


def fast_shards(n, m, proj_in, taps, long_filter, out_grad):
    streams, rows, channels = proj_in.shape
    groups = long_filter.shape[1]
    reps = channels // groups
    part = rows // reps
    tokens = n * rows
    half = tokens // 2
    tiles = n // reps
    f32, bf16 = jnp.float32, jnp.bfloat16
    shape, vmem = jax.ShapeDtypeStruct, pltpu.VMEM
    share = part // m
    quarters = vmem((m, n, share, LANES), f32)
    quarter = vmem((n, share, LANES), f32)
    moved = vmem((2, n, rows, LANES), bf16)
    rims = vmem((n, 16, LANES), bf16)
    features = vmem((rows, channels), f32)
    both = vmem((half, 2 * LANES), bf16)
    spectrum = vmem((4, half, LANES), f32)
    products = vmem((tokens, 2 * LANES), bf16)
    edges = vmem((2, n * 8, LANES), f32)
    packed = vmem((n, part, LANES), bf16)
    out, long_grad, tap_grad = pl.pallas_call(
        functools.partial(whole_kernel, n, m, reps),
        out_shape=(
            vmem((streams, rows, channels), bf16), vmem((groups // m, rows), f32), vmem(taps.shape, f32),
        ),
        in_specs=[pl.BlockSpec(memory_space=pl.ANY)] * 5,
        out_specs=whole_specs(3),
        scratch_shapes=[vmem(proj_in.shape, bf16), vmem(out_grad.shape, bf16)]
        + [vmem(long_filter.shape, f32), vmem(taps.shape, f32)]
        + [vmem((TABLES + 1, half, half), bf16), vmem((16, channels), f32), rims, rims]
        + [vmem((n * 16, LANES), f32), moved, moved, features, features]
        + [packed, packed, vmem((tokens, LANES), f32), both, both]
        + [spectrum, spectrum] + [products] * 6 + [vmem((2, half, LANES), f32)] * 2
        + [vmem((2, 2, n // 2, rows, LANES), bf16), moved, edges, edges]
        + [quarters, quarters, quarter, quarter, vmem((m, n // m, share, LANES), f32)]
        + [vmem((64, LANES), f32), vmem((64, LANES), bf16), vmem((n, 64, LANES), bf16)]
        + [vmem((tiles, 16, LANES), f32), vmem((tiles, 16, LANES), bf16), vmem((tiles, n, 16, LANES), bf16)]
        + [pltpu.SemaphoreType.DMA((8,)), pltpu.SemaphoreType.DMA((2, 12, n - 1))]
        + [pltpu.SemaphoreType.DMA((2, 2, m - 1))],
        compiler_params=pltpu.CompilerParams(
            collective_id=0, has_side_effects=True, vmem_limit_bytes=56 << 20
        ),
    )(proj_in, out_grad, long_filter, taps, tables_of(tokens, swap_matrix(reps, LANES // reps)))
    out, long_grad, tap_grad = pl.pallas_call(
        hand_over,
        out_shape=tuple(shape(x.shape, x.dtype) for x in (out, long_grad, tap_grad)),
        in_specs=[pl.BlockSpec(memory_space=pl.ANY)] * 3,
        out_specs=[pl.BlockSpec(memory_space=pl.ANY)] * 3,
        scratch_shapes=[pltpu.SemaphoreType.DMA((3,))],
        compiler_params=pltpu.CompilerParams(vmem_limit_bytes=1 << 20),
    )(out, long_grad, tap_grad)
    return (out, long_grad.T, tap_grad)


def fits(n, m, proj_in, taps, long_filter, out_grad):
    streams, rows, channels = proj_in.shape
    groups = long_filter.shape[1]
    if channels % groups or groups % n or n % m or streams != 3 or taps.shape[1] != 3:
        return False
    reps, width = channels // groups, groups // n
    if reps < 2 or reps * width != LANES or n % reps or rows % (8 * reps * m) or rows % LANES:
        return False
    if reps * LANES != n * rows // 2:
        return False
    if n % 8 or reps * 3 + RIM > 16 or 6 * n + RIM > 64 or rows // reps % 16 or n // 2 % reps:
        return False
    return n * rows <= TABLE_LIMIT and n * rows % 1024 == 0


def routed(n, m, *arrays):
    return fast_shards(n, m, *arrays) if fits(n, m, *arrays) else shards(*arrays)


def solution(mesh):
    return jax.shard_map(
        functools.partial(routed, mesh.shape["seq"], mesh.shape["chan"]),
        mesh=mesh,
        in_specs=(P(None, "seq", "chan"), P(None, None, "chan"), P("seq", None), P("seq", "chan")),
        out_specs=(P(None, "seq", "chan"), P("seq", "chan"), P(None, None, "chan")),
        check_vma=False,
    )
```

```python
import functools
import math

import jax
import jax.numpy as jnp
import numpy as np
from jax import lax
from jax.experimental import pallas as pl
from jax.experimental.pallas import tpu as pltpu
from jax.sharding import PartitionSpec as P

MESH = pl.DeviceIdType.MESH
LANES = 128
TABLE_LIMIT = 1024
LEVELS = 250.0
RIM = 2
TABLES = 12


def shifted(x, axis, by):
    devices = lax.axis_size(axis)
    pairs = [(i, i + by) for i in range(devices) if 0 <= i + by < devices]
    return lax.ppermute(x, axis, pairs)


def angle_table(left_index, right_index, period):
    product = left_index[:, None] * right_index[None, :] % period
    phase = product.astype(jnp.float32) * (2.0 * math.pi / period)
    return (jnp.cos(phase), jnp.sin(phase))


def contract(pattern, factor_table, operand):
    return jnp.einsum(pattern, factor_table, operand, precision=lax.Precision.HIGHEST)


def steps_of(count):
    return jnp.arange(count, dtype=jnp.int32)


def whole_forward(signal, seq_width):
    tok_rows, stack_count, channels = signal.shape
    period = 2 * seq_width * tok_rows
    narrow = channels // seq_width
    arrived = lax.all_to_all(signal, "seq", split_axis=2, concat_axis=0, tiled=True)
    laid = arrived.reshape(seq_width, tok_rows, stack_count, narrow).transpose(2, 3, 0, 1)
    cos_step, sin_step = angle_table(steps_of(2 * seq_width), steps_of(seq_width), 2 * seq_width)
    real_part = contract("qm,ncmj->ncqj", cos_step, laid)
    imag_part = -contract("qm,ncmj->ncqj", sin_step, laid)
    cos_turn, sin_turn = angle_table(steps_of(2 * seq_width), steps_of(tok_rows), period)
    turned_re = real_part * cos_turn + imag_part * sin_turn
    turned_im = imag_part * cos_turn - real_part * sin_turn
    cos_row, sin_row = angle_table(steps_of(tok_rows), steps_of(tok_rows), tok_rows)
    spec_re = contract("rj,ncqj->ncqr", cos_row, turned_re) + contract(
        "rj,ncqj->ncqr", sin_row, turned_im
    )
    spec_im = contract("rj,ncqj->ncqr", cos_row, turned_im) - contract(
        "rj,ncqj->ncqr", sin_row, turned_re
    )
    return (spec_re, spec_im)


def whole_inverse(spec_re, spec_im, seq_width):
    stack_count, narrow, freq_count, tok_rows = spec_re.shape
    period = 2 * seq_width * tok_rows
    cos_row, sin_row = angle_table(steps_of(tok_rows), steps_of(tok_rows), tok_rows)
    back_re = contract("rj,ncqr->ncqj", cos_row, spec_re) - contract(
        "rj,ncqr->ncqj", sin_row, spec_im
    )
    back_im = contract("rj,ncqr->ncqj", sin_row, spec_re) + contract(
        "rj,ncqr->ncqj", cos_row, spec_im
    )
    cos_turn, sin_turn = angle_table(steps_of(freq_count), steps_of(tok_rows), period)
    turned_re = back_re * cos_turn - back_im * sin_turn
    turned_im = back_re * sin_turn + back_im * cos_turn
    cos_step, sin_step = angle_table(steps_of(seq_width), steps_of(freq_count), freq_count)
    signal = contract("mq,ncqj->ncmj", cos_step, turned_re) - contract(
        "mq,ncqj->ncmj", sin_step, turned_im
    )
    signal = (
        (signal / period).transpose(2, 3, 0, 1).reshape(seq_width * tok_rows, stack_count, narrow)
    )
    return lax.all_to_all(signal, "seq", split_axis=0, concat_axis=2, tiled=True)


def member(values, index, stack_axis):
    return lax.index_in_dim(values, index, stack_axis, keepdims=False)


def shards(proj_in, taps, long_filter, out_grad):
    stream_count, tok_rows, channels = proj_in.shape
    tap_count = taps.shape[1]
    groups = long_filter.shape[1]
    seq_width = lax.axis_size("seq")
    lower_rim = shifted(proj_in[:, tok_rows - (tap_count - 1) :, :], "seq", 1)
    extended = jnp.concatenate([lower_rim, proj_in], axis=1).astype(jnp.float32)
    lagged = [
        extended[:, tap_count - 1 - lag_step : tap_count - 1 - lag_step + tok_rows, :]
        for lag_step in range(tap_count)
    ]
    featured = taps[:, 0, None, :] * lagged[0]
    for lag_step in range(1, tap_count):
        featured = featured + taps[:, lag_step, None, :] * lagged[lag_step]
    query_rows, key_rows, value_rows = (featured[0], featured[1], featured[2])
    mixed_rows = key_rows * value_rows
    upstream = out_grad.astype(jnp.float32)
    conv_grad = upstream * query_rows
    tiled_filter = jnp.tile(long_filter, (1, channels // groups))
    signals = jnp.stack([mixed_rows, conv_grad, tiled_filter], axis=1)
    data_re, data_im = whole_forward(signals, seq_width)
    stack_axis = 0
    mix_re, mix_im = (member(data_re, 0, stack_axis), member(data_im, 0, stack_axis))
    grad_re, grad_im = (member(data_re, 1, stack_axis), member(data_im, 1, stack_axis))
    filt_re, filt_im = (member(data_re, 2, stack_axis), member(data_im, 2, stack_axis))
    conv_re = filt_re * mix_re - filt_im * mix_im
    conv_im = filt_re * mix_im + filt_im * mix_re
    back_re = filt_re * grad_re + filt_im * grad_im
    back_im = filt_re * grad_im - filt_im * grad_re
    corr_re = grad_re * mix_re + grad_im * mix_im
    corr_im = grad_im * mix_re - grad_re * mix_im
    prod_re = jnp.stack([conv_re, back_re, corr_re], axis=stack_axis)
    prod_im = jnp.stack([conv_im, back_im, corr_im], axis=stack_axis)
    outputs = whole_inverse(prod_re, prod_im, seq_width)
    conv_out, mixed_grad = (outputs[:, 0], outputs[:, 1])
    filt_grad = jnp.sum(outputs[:, 2].reshape(tok_rows, channels // groups, groups), axis=1)
    long_grad = lax.psum_scatter(filt_grad, "chan", scatter_dimension=1, tiled=True)
    feature_grad = jnp.stack(
        [upstream * conv_out, mixed_grad * value_rows, mixed_grad * key_rows], axis=0
    )
    upper_rim = shifted(feature_grad[:, : tap_count - 1, :], "seq", -1)
    trailing = jnp.concatenate([feature_grad, upper_rim], axis=1)
    input_grad = taps[:, 0, None, :] * feature_grad
    for lag_step in range(1, tap_count):
        input_grad = (
            input_grad + taps[:, lag_step, None, :] * trailing[:, lag_step : lag_step + tok_rows]
        )
    partial_taps = jnp.stack(
        [jnp.sum(feature_grad * lagged[lag_step], axis=1) for lag_step in range(tap_count)], axis=1
    )
    tap_grad = lax.psum(partial_taps, "seq") / math.sqrt(seq_width * tok_rows)
    return (input_grad.astype(jnp.bfloat16), long_grad, tap_grad)


def greet(axis_sizes):
    barrier = pltpu.get_barrier_semaphore()
    for axis, size in axis_sizes:
        me = lax.axis_index(axis)
        for j in range(1, size):
            pl.semaphore_signal(
                barrier, inc=1, device_id={axis: lax.rem(me + j, size)}, device_id_type=MESH
            )


def welcome(sizes):
    pl.semaphore_wait(pltpu.get_barrier_semaphore(), sum(size - 1 for size in sizes))


def swap_matrix(reps, width):
    side = reps * LANES
    row, col = np.arange(side)[:, None], np.arange(side)[None, :]
    outer, inner, rest = row // LANES, (row % LANES) // width, row % width
    return (inner * LANES + outer * width + rest == col).astype(jnp.bfloat16)


def lane_group(rows, width):
    return lax.broadcasted_iota(jnp.int32, (rows, LANES), 1) // width


def row_of(shape):
    return lax.broadcasted_iota(jnp.int32, shape, 0)


def turn(x, shift, axis):
    shift = shift % x.shape[axis]
    return x if shift == 0 else pltpu.roll(x, shift, axis)


def halves(x):
    high = x.astype(jnp.bfloat16)
    return high, (x - high.astype(jnp.float32)).astype(jnp.bfloat16)


def later(x):
    return jnp.where(row_of(x.shape) < 1, 0.0, pltpu.roll(x, 1, 0))


def sooner(x):
    rows = x.shape[0]
    return jnp.where(row_of(x.shape) >= rows - 1, 0.0, pltpu.roll(x, rows - 1, 0))


def group_sum(x, reps):
    step = LANES // reps
    if reps & (reps - 1):
        return sum((turn(x, r * step, 1) for r in range(1, reps)), x)
    while step < LANES:
        x = x + turn(x, step, 1)
        step *= 2
    return x


def scale_of(size):
    top = jnp.max(size, axis=0, keepdims=True)
    return jnp.maximum(top * (1.0 + 2.0**-7), 1e-30).astype(jnp.bfloat16).astype(jnp.float32)


def code_of(x, size, scale):
    level = jnp.exp2(size * (LEVELS / scale) - 0.5 * LEVELS)
    return jnp.where(x < 0.0, -level, level)


def encode(x):
    size = jnp.abs(x)
    first = jnp.where(row_of((8, LANES)) < RIM, 0.0, size[:8])
    scale = scale_of(jnp.concatenate([first, size[8:]], axis=0))
    level = code_of(x, size, scale)
    first = jnp.where(row_of((8, LANES)) < RIM, scale, level[:8])
    return jnp.concatenate([first, level[8:]], axis=0).astype(jnp.bfloat16)


def decode(code, scale=None):
    scale = code[:1] if scale is None else scale
    size = (jnp.log(jnp.abs(code)) * (1.0 / (math.log(2.0) * LEVELS)) + 0.5) * scale
    return jnp.where(code < 0.0, -size, size)


def dot(left, right):
    return jnp.dot(left, right, preferred_element_type=jnp.float32)


def three(high, low, x_high, x_low):
    return dot(high, x_high) + (dot(high, x_low) + dot(low, x_high))


def paired(high, low, both):
    wide = dot(high, both)
    return wide[:, :LANES] + (wide[:, LANES:] + dot(low, both[:, :LANES]))


def alternating(count):
    return jnp.where(row_of((count, LANES)) % 2 == 0, 1.0, -1.0)


def whole_kernel(
    n, m, reps, x_hbm, og_hbm, lf_hbm, tp_hbm, tb_hbm, out_ref, lo_ref, to_ref,
    x_ref, og_ref, lf_ref, tp_ref, tb, ex, es, er, exf, xs, xr, kf, vf, fs, fr, buf, both_e, both_o, fsp, gsp, pq_e, pq_o, eh, el, oh, ol,
    half_out, corr, codes, igr, back, backr, lgs, lgc, lsum, lgr, l2, ts, tc, tg, us, uc, ug, lsem, sems, csems,
):
    me, mine = lax.axis_index("seq"), lax.axis_index("chan")
    width = LANES // reps
    streams, rows, _ = x_ref.shape
    tap_count = tp_ref.shape[1]
    tokens = n * rows
    half = tokens // 2
    near = n // 2
    part = rows // reps
    share = part // m
    tiles = n // reps
    f32, bf16 = jnp.float32, jnp.bfloat16
    pairs = [
        (lf_hbm, lf_ref), (og_hbm, og_ref), (x_hbm.at[0], x_ref.at[0]), (tp_hbm, tp_ref),
        (tb_hbm.at[TABLES], tb.at[TABLES]), (x_hbm.at[1], x_ref.at[1]), (x_hbm.at[2], x_ref.at[2]),
        (tb_hbm.at[:TABLES], tb.at[:TABLES]),
    ]
    fetched = [pltpu.make_async_copy(*pair, lsem.at[i]) for i, pair in enumerate(pairs)]
    for copy in fetched:
        copy.start()
    sw_ref = tb.at[TABLES]
    grp = lane_group(part, width)
    greet([("seq", n), ("chan", m)])
    fetched[0].wait()
    scales = []

    def remote(kind, slot, source, target, peer):
        copy = pltpu.make_async_remote_copy(
            src_ref=source, dst_ref=target, send_sem=sems.at[0, kind, slot],
            recv_sem=sems.at[1, kind, slot], device_id={"seq": peer}, device_id_type=MESH,
        )
        copy.start()
        return copy

    def ship(kind, source, target):
        return [
            remote(kind, j - 1, source(lax.rem(me + j, n)), target, lax.rem(me + j, n))
            for j in sorted(range(1, n), key=lambda j: abs(2 * j - n))
        ]

    def spread(kind, source, target):
        copies = []
        for j in range(1, m):
            peer = lax.rem(mine + j, m)
            copy = pltpu.make_async_remote_copy(
                src_ref=source(peer), dst_ref=target, send_sem=csems.at[0, kind, j - 1],
                recv_sem=csems.at[1, kind, j - 1], device_id={"chan": peer}, device_id_type=MESH,
            )
            copy.start()
            copies.append(copy)
        return copies

    def place(r, h):
        return pl.ds(pl.multiple_of((r * tiles + h) * LANES, LANES), LANES)

    def feature(p, at):
        x = x_ref[p, :, at].astype(f32)
        total = tp_ref[p, 0:1, at] * x
        for lag in range(1, tap_count):
            total = total + tp_ref[p, lag : lag + 1, at] * pltpu.roll(x, lag, 0)
        return total

    def send_layout(pieces, place_at):
        moved = dot(jnp.concatenate(pieces, axis=1), sw_ref[...]).astype(bf16)
        for g in range(reps):
            place_at(g)[...] = moved[:, g * LANES : (g + 1) * LANES]

    for s in range(n):
        base = (s // reps) * LANES
        packed = jnp.zeros((part, LANES), f32)
        for q in range(reps):
            tile = lf_ref[q * part : (q + 1) * part, base : base + LANES]
            packed = jnp.where(grp == q, turn(tile, (q - s % reps) * width, 1), packed)
        size = jnp.abs(packed)
        scales.append(scale_of(size))
        fs[s] = code_of(packed, size, scales[s]).astype(bf16)
    for copy in fetched[1:-1]:
        copy.wait()
    ex[...] = jnp.zeros_like(ex)
    for p in range(streams):
        ex[RIM * p : RIM * (p + 1), :] = x_ref[p, :16, :].astype(f32)[:RIM]
        ex[8 + RIM * p : 8 + RIM * (p + 1), :] = x_ref[p, rows - 16 :, :].astype(f32)[16 - RIM :]
    ex[RIM * streams : RIM * (streams + 1), :] = og_ref[:16, :].astype(f32)[:RIM]
    for h in range(tiles):
        joined = jnp.concatenate([ex[:, place(r, h)].astype(bf16) for r in range(reps)], axis=1)
        moved = dot(joined, sw_ref[...])
        for g in range(reps):
            block = moved[:, g * LANES : (g + 1) * LANES]
            block = jnp.where(row_of((16, LANES)) == 14, scales[h * reps + g], block)
            es[h * reps + g] = block.astype(bf16)
    side = me // near

    def prepare(plane, piece, step):
        which = (1 - side) if step == 0 else side
        for k in range(near // reps):
            h = which * (near // reps) + k
            send_layout([piece(place(r, h)) for r in range(reps)], lambda g: xs.at[plane, h * reps + g])

    def send_mixed(kind, plane):
        copies = []
        for i in range(near):
            for step in range(2):
                if i < step:
                    continue
                which = (1 - side) if step == 0 else side
                peer = which * near + lax.rem(me + i, near)
                copies.append(
                    remote(kind, step * near + i - step, xs.at[plane, peer], xr.at[plane, me], peer)
                )
        return copies

    def mixed_piece(at):
        key, value = feature(1, at), feature(2, at)
        kf[:, at], vf[:, at] = key, value
        return encode(key * value)

    for step in range(2):
        prepare(0, lambda at: encode(og_ref[:, at].astype(f32) * feature(0, at)), step)
    welcome([n, m])
    filter_sent = ship(0, lambda peer: fs.at[peer], fr.at[me])
    rims_sent = ship(1, lambda peer: es.at[peer], er.at[me])
    first = send_mixed(2, 0)
    for step in range(2):
        prepare(1, mixed_piece, step)
    second = send_mixed(3, 1)
    fr[me] = fs[me]
    er[me] = es[me]
    xr[0, me] = xs[0, me]
    xr[1, me] = xs[1, me]

    taps = []
    home, slot = me // reps, lax.rem(me, reps)
    for p in range(streams):
        mixed_taps = jnp.zeros((tap_count, LANES), f32)
        for r in range(reps):
            at = pl.multiple_of((r * tiles + home) * LANES, LANES)
            tile = tp_ref[p, :, pl.ds(at, LANES)]
            shift = lax.rem((r + reps - slot) * width, LANES)
            mixed_taps = jnp.where(
                lane_group(tap_count, width) == r, pltpu.roll(tile, shift, 1), mixed_taps
            )
        taps.append([mixed_taps[i : i + 1] for i in range(tap_count)])

    def split():
        ends = []
        for part_of, both in ((0, both_e), (1, both_o)):
            values = buf[pl.ds(part_of, half, stride=2), :]
            both[:, :LANES], both[:, LANES:] = halves(values)
            ends.append(jnp.sum(alternating(half) * values, axis=0, keepdims=True))
        return ends

    chunk = min(256, half)

    def spectra(at):
        return [
            paired(tb[2 * table + 0, at, :], tb[2 * table + 1, at, :], both[...])
            for table, both in ((0, both_e), (1, both_e), (2, both_o), (3, both_o))
        ]

    def store_products(at, low, even_cos, even_sin, odd_cos, odd_sin):
        pq_e[at, :LANES], pq_e[at, LANES:] = halves(even_cos)
        pq_e[low, :LANES], pq_e[low, LANES:] = halves(even_sin)
        pq_o[at, :LANES], pq_o[at, LANES:] = halves(odd_cos)
        pq_o[low, :LANES], pq_o[low, LANES:] = halves(odd_sin)

    def inverse(at, end_e, end_o):
        even = paired(tb[0, at, :], tb[1, at, :], pq_e[:half])
        even = even + paired(tb[2, at, :], tb[3, at, :], pq_e[half:])
        odd = paired(tb[8, at, :], tb[9, at, :], pq_o[:half])
        odd = odd + paired(tb[10, at, :], tb[11, at, :], pq_o[half:])
        sign = alternating(chunk)
        return [even + sign * end_e], [odd + sign * end_o]

    def inverse_both(at, end_e, end_o):
        even = three(tb[0, at, :], tb[1, at, :], eh[:half], el[:half])
        even = even + three(tb[2, at, :], tb[3, at, :], eh[half:], el[half:])
        odd = three(tb[8, at, :], tb[9, at, :], oh[:half], ol[:half])
        odd = odd + three(tb[10, at, :], tb[11, at, :], oh[half:], ol[half:])
        sign = alternating(chunk)
        lanes = (slice(0, LANES), slice(LANES, 2 * LANES))
        return tuple(
            [value[:, lane] + sign * end[k] for k, lane in enumerate(lanes)]
            for value, end in ((even, end_e), (odd, end_o))
        )

    def return_layout(kind, inverse_of, end_e, end_o, between=lambda: None):
        copies = []
        for step in range(2):
            which = (1 - side) if step == 0 else side
            for c in range(half // 2 // chunk):
                at = pl.ds(pl.multiple_of(which * (half // 2) + c * chunk, chunk), chunk)
                for offset, values in enumerate(inverse_of(at, end_e, end_o)):
                    for value, place_of in zip(values, (half_out, corr)):
                        place_of[step, pl.ds(2 * c * chunk + offset, chunk, stride=2), :] = value
            for i in range(near):
                codes[kind, step, i] = encode(half_out[step, i * rows : (i + 1) * rows, :])
            if step == 1:
                between()
            for i in range(step, near):
                inner = lax.rem(me + i, near)
                copies.append(
                    remote(
                        4 + 2 * kind, step * near + i - step, codes.at[kind, step, inner],
                        igr.at[kind, me], which * near + inner,
                    )
                )
        igr[kind, me] = codes[kind, 1, lax.rem(me, near)]
        rims = []
        for i in range(RIM):
            far_rows = half_out[0, pl.ds(i, near, stride=rows), :]
            near_rows = half_out[1, pl.ds(i, near, stride=rows), :]
            low = jnp.where(side == 0, near_rows, far_rows)
            high = jnp.where(side == 0, far_rows, near_rows)
            rims.append(jnp.concatenate([low, high], axis=0))
        return copies, rims

    def return_rims(kind, grads):
        if len(grads) == 1:
            back[kind, ...] = jnp.zeros_like(back[kind])
        for k, pair in enumerate(grads):
            for i in range(RIM):
                back[kind, pl.ds(RIM * k + i, n, stride=8), :] = pair[i]
                back[kind, pl.ds(RIM * (k + len(grads)) + i, n, stride=8), :] = sooner(pair[i])
        mine_at = pl.ds(pl.multiple_of(me * 8, 8), 8)
        backr[kind, mine_at, :] = back[kind, mine_at, :]
        copies = []
        for step in range(2):
            which = (1 - side) if step == 0 else side
            for i in range(step, near):
                peer = which * near + lax.rem(me + i, near)
                source = back.at[kind, pl.ds(pl.multiple_of(peer * 8, 8), 8)]
                copies.append(
                    remote(5 + 2 * kind, step * near + i - step, source, backr.at[kind, mine_at], peer)
                )
        return copies

    for copy in filter_sent + rims_sent:
        copy.wait()
    exf[...] = er[...].reshape(n * 16, LANES).astype(f32)

    def rim(i):
        return exf[pl.ds(i, n, stride=16), :]

    def rim_feature(p):
        now, before = [rim(RIM * p), rim(RIM * p + 1)], [rim(8 + RIM * p + 1), rim(8 + RIM * p)]
        near_rows = [now[1], now[0], later(before[0]), later(before[1])]
        out = []
        for i in range(RIM):
            total = taps[p][0] * near_rows[1 - i]
            for lag in range(1, tap_count):
                total = total + taps[p][lag] * near_rows[1 - i + lag]
            out.append(total)
        return out

    query_rim, key_rim, value_rim = (rim_feature(p) for p in range(streams))
    grad_rim = [rim(RIM * streams), rim(RIM * streams + 1)]

    def collect(k, rims):
        for s in range(n):
            buf[s * rows : (s + 1) * rows, :] = decode(xr[k, s].astype(f32))
        for i in range(RIM):
            buf[pl.ds(i, n, stride=rows), :] = rims[i]

    for s in range(n):
        packed = decode(fr[s].astype(f32), exf[16 * s + 14 : 16 * s + 15, :])
        for q in range(reps):
            at = s * rows + q * part
            buf[at : at + part, :] = group_sum(jnp.where(grp == q, packed, 0.0), reps)
    filt_e, filt_o = split()
    fetched[-1].wait()

    @pl.loop(0, half // chunk)
    def _(i):
        at = pl.ds(pl.multiple_of(i * chunk, chunk), chunk)
        weight = jnp.where(row_of((chunk, LANES)) + i * chunk == 0, 1.0 / tokens, 2.0 / tokens)
        for k, value in enumerate(spectra(at)):
            fsp[k, at, :] = value * weight

    for copy in first:
        copy.wait()
    collect(0, [grad_rim[i] * query_rim[i] for i in range(RIM)])
    grad_e, grad_o = split()

    @pl.loop(0, half // chunk)
    def _(i):
        at = pl.ds(pl.multiple_of(i * chunk, chunk), chunk)
        low = pl.ds(pl.multiple_of(half + i * chunk, chunk), chunk)
        ge, te, go, to = spectra(at)
        for k, value in enumerate((ge, te, go, to)):
            gsp[k, at, :] = value
        fe, se, fo, so = (fsp[k, at, :] for k in range(4))
        store_products(
            at, low,
            fe * ge + fo * go + se * te + so * to,
            fe * te + fo * to - se * ge - so * go,
            fe * go + fo * ge + se * to + so * te,
            fe * to + fo * te - se * go - so * ge,
        )

    back_sent, back_rim = return_layout(
        0, inverse, (filt_e * grad_e + filt_o * grad_o) * (1.0 / tokens),
        (filt_e * grad_o - filt_o * grad_e) * (1.0 / tokens),
    )
    back_rims_sent = return_rims(
        0, [[back_rim[i] * value_rim[i] for i in range(RIM)], [back_rim[i] * key_rim[i] for i in range(RIM)]]
    )

    for copy in second:
        copy.wait()
    collect(1, [key_rim[i] * value_rim[i] for i in range(RIM)])
    mixed_e, mixed_o = split()

    @pl.loop(0, half // chunk)
    def _(i):
        at = pl.ds(pl.multiple_of(i * chunk, chunk), chunk)
        low = pl.ds(pl.multiple_of(half + i * chunk, chunk), chunk)
        he, ye, ho, yo = spectra(at)
        fe, se, fo, so = (fsp[k, at, :] for k in range(4))
        ge, te, go, to = (gsp[k, at, :] for k in range(4))
        weight = jnp.where(row_of((chunk, LANES)) + i * chunk == 0, 1.0 / tokens, 2.0 / tokens)

        def put(high, low_part, rows_at, conv, cross):
            high[rows_at, :LANES], low_part[rows_at, :LANES] = halves(conv)
            high[rows_at, LANES:], low_part[rows_at, LANES:] = halves(cross * weight)

        put(
            eh, el, at, fe * he + fo * ho - se * ye - so * yo,
            ge * he + go * ho + te * ye + to * yo,
        )
        put(
            eh, el, low, fe * ye + fo * yo + se * he + so * ho,
            te * he + to * ho - ge * ye - go * yo,
        )
        put(
            oh, ol, at, fe * ho + fo * he - se * yo - so * ye,
            ge * ho + go * he + te * yo + to * ye,
        )
        put(
            oh, ol, low, fe * yo + fo * ye + se * ho + so * he,
            te * ho + to * he - ge * yo - go * ye,
        )

    long_parts = []

    def filter_terms():
        for s in range(n):
            packed = jnp.zeros((part, LANES), f32)
            for q in range(reps):
                at = s % near * rows + q * part
                step = jnp.where(side == s // near, 1, 0)
                packed = jnp.where(grp == q, group_sum(corr[step, at : at + part, :], reps), packed)
            for k in range(m):
                lgs[k, s] = packed[k * share : (k + 1) * share]
        long_parts.extend(spread(1, lambda peer: lgs.at[peer], lgc.at[mine]))
        lgc[mine] = lgs[mine]

    inv = 1.0 / tokens
    conv_sent, conv_rim = return_layout(
        1, inverse_both,
        ((filt_e * mixed_e - filt_o * mixed_o) * inv, (grad_e * mixed_e + grad_o * mixed_o) * inv),
        ((filt_e * mixed_o + filt_o * mixed_e) * inv, (grad_o * mixed_e - grad_e * mixed_o) * inv),
        filter_terms,
    )
    conv_rims_sent = return_rims(1, [[conv_rim[i] * grad_rim[i] for i in range(RIM)]])

    def own_rims(kind, h, r):
        line = jnp.zeros((8, LANES), f32)
        for g in range(reps):
            at = pl.ds(pl.multiple_of((h * reps + g) * 8, 8), 8)
            moved = turn(backr[kind, at, :], (g - r) * width, 1)
            line = jnp.where(lane_group(8, width) == g, moved, line)
        return line

    def own_codes(kind, h):
        return dot(jnp.concatenate([igr[kind, h * reps + g] for g in range(reps)], axis=1), sw_ref[...])

    def finish(p, at, grads, own, after):
        row8 = row_of((8, LANES))
        first_rows = jnp.where(row8 == 0, own[0:1], jnp.where(row8 == 1, own[1:2], grads[:8]))
        grads = jnp.concatenate([first_rows, grads[8:]], axis=0)
        one, two = pltpu.roll(grads, rows - 1, 0), pltpu.roll(grads, rows - 2, 0)
        last = jnp.where(row8 == 7, after[0:1], one[rows - 8 :])
        one = jnp.concatenate([one[: rows - 8], last], axis=0)
        last = jnp.where(row8 == 7, after[1:2], jnp.where(row8 == 6, after[0:1], two[rows - 8 :]))
        two = jnp.concatenate([two[: rows - 8], last], axis=0)
        x = x_ref[p, :, at].astype(f32)
        total, lines = None, []
        for lag, value in enumerate((grads, one, two)):
            term = tp_ref[p, lag : lag + 1, at] * value
            total = term if total is None else total + term
            lines.append(jnp.sum(x * value, axis=0, keepdims=True) * (1.0 / math.sqrt(tokens)))
        out_ref[p, :, at] = total.astype(bf16)
        return lines

    for copy in long_parts:
        copy.wait()
    lsum[...] = sum((lgc[k] for k in range(1, m)), lgc[0])
    long_sent = ship(9, lambda peer: lsum.at[peer], lgr.at[me])
    lgr[me] = lsum[me]
    for copy in back_sent:
        copy.wait()
    for copy in back_rims_sent:
        copy.wait()
    ts[...] = jnp.zeros_like(ts)
    for h in range(tiles):
        moved = own_codes(0, h)
        for r in range(reps):
            at = place(r, h)
            grads = decode(moved[:, r * LANES : (r + 1) * LANES])
            edge = own_rims(0, h, r)
            for p, other in ((1, vf), (2, kf)):
                k = RIM * (p - 1)
                lines = finish(
                    p, at, grads * other[:, at], edge[k : k + RIM], edge[k + 4 : k + 4 + RIM]
                )
                for lag in range(tap_count):
                    at_row = RIM + (r * tiles + h) * 2 * tap_count + tap_count * (p - 1) + lag
                    ts[at_row : at_row + 1, :] = lines[lag]
    tc[...] = encode(ts[...])
    taps_sent = ship(8, lambda peer: tc, tg.at[me])
    tg[me] = tc[...]
    per = n // m

    us[...] = jnp.zeros_like(us)
    query_sent = []

    def arriving(step):
        part_of = slice(near, None) if step == 0 else slice(0, near)
        return conv_sent[part_of] + conv_rims_sent[part_of]

    for step in range(2):
        for copy in arriving(step):
            copy.wait()
        h = side if step == 0 else 1 - side
        moved = own_codes(1, h)
        for r in range(reps):
            at = place(r, h)
            grads = decode(moved[:, r * LANES : (r + 1) * LANES]) * og_ref[:, at].astype(f32)
            edge = own_rims(1, h, r)
            lines = finish(0, at, grads, edge[:RIM], edge[RIM : 2 * RIM])
            for lag in range(tap_count):
                at_row = RIM + tap_count * r + lag
                us[h, at_row : at_row + 1, :] = lines[lag]
        uc[h] = encode(us[h])
        query_sent.append(ship(10 + step, lambda peer: uc.at[h], ug.at[h, me]))
        ug[h, me] = uc[h]
    for copy in long_sent:
        copy.wait()
    chan_sent = spread(0, lambda peer: lgr.at[pl.ds(peer * per, per)], l2.at[mine])
    l2[mine] = lgr[pl.ds(mine * per, per)]
    for copy in taps_sent:
        copy.wait()
    ts[...] = sum((decode(tg[s].astype(f32)) for s in range(1, n)), decode(tg[0].astype(f32)))
    for t in range(n):
        for p in (1, 2):
            at = RIM + 2 * tap_count * t + tap_count * (p - 1)
            to_ref[p, :, t * LANES : (t + 1) * LANES] = ts[at : at + tap_count, :]
    for copy in chan_sent:
        copy.wait()
    sources = [jnp.concatenate([l2[q, k] for q in range(m)], axis=0) for k in range(per)]
    lines = []
    for q in range(reps):
        line = jnp.zeros((part, LANES), f32)
        for k in range(per):
            line = jnp.where(grp == k, turn(sources[k], (k - q) * width, 1), line)
        lines.append(line)
    lo_ref[...] = jnp.concatenate(lines, axis=0).T[: per * width]
    for copy in query_sent[0] + query_sent[1]:
        copy.wait()
    for h in range(tiles):
        us[h] = sum((decode(ug[h, s].astype(f32)) for s in range(1, n)), decode(ug[h, 0].astype(f32)))
        for r in range(reps):
            at = RIM + tap_count * r
            to_ref[0, :, place(r, h)] = us[h, at : at + tap_count, :]


def hand_over(out_from, long_from, tap_from, out_to, long_to, tap_to, sem):
    pairs = ((out_from, out_to), (tap_from, tap_to), (long_from, long_to))
    copies = [pltpu.make_async_copy(*pair, sem.at[i]) for i, pair in enumerate(pairs)]
    for copy in copies:
        copy.start()
    for copy in copies:
        copy.wait()


def whole_specs(count):
    return [pl.BlockSpec(memory_space=pltpu.VMEM)] * count


def tables_of(tokens, swap):
    half = tokens // 2
    freq, step = np.arange(half)[:, None], np.arange(half)[None, :]
    even = freq * (2 * step) % (2 * tokens) * (math.pi / tokens)
    odd = freq * (2 * step + 1) % (2 * tokens) * (math.pi / tokens)
    tables = [np.cos(even), np.sin(even), np.cos(odd), np.sin(odd), np.cos(odd).T, np.sin(odd).T]
    out = []
    for table in tables:
        high = table.astype(np.float32).astype(jnp.bfloat16)
        low = (table - high.astype(np.float64)).astype(np.float32).astype(jnp.bfloat16)
        out += [high, low]
    return np.stack(out + [swap])


def fast_shards(n, m, proj_in, taps, long_filter, out_grad):
    streams, rows, channels = proj_in.shape
    groups = long_filter.shape[1]
    reps = channels // groups
    part = rows // reps
    tokens = n * rows
    half = tokens // 2
    tiles = n // reps
    f32, bf16 = jnp.float32, jnp.bfloat16
    shape, vmem = jax.ShapeDtypeStruct, pltpu.VMEM
    share = part // m
    quarters = vmem((m, n, share, LANES), f32)
    quarter = vmem((n, share, LANES), f32)
    moved = vmem((2, n, rows, LANES), bf16)
    rims = vmem((n, 16, LANES), bf16)
    features = vmem((rows, channels), f32)
    both = vmem((half, 2 * LANES), bf16)
    spectrum = vmem((4, half, LANES), f32)
    products = vmem((tokens, 2 * LANES), bf16)
    edges = vmem((2, n * 8, LANES), f32)
    packed = vmem((n, part, LANES), bf16)
    out, long_grad, tap_grad = pl.pallas_call(
        functools.partial(whole_kernel, n, m, reps),
        out_shape=(
            vmem((streams, rows, channels), bf16), vmem((groups // m, rows), f32), vmem(taps.shape, f32),
        ),
        in_specs=[pl.BlockSpec(memory_space=pl.ANY)] * 5,
        out_specs=whole_specs(3),
        scratch_shapes=[vmem(proj_in.shape, bf16), vmem(out_grad.shape, bf16)]
        + [vmem(long_filter.shape, f32), vmem(taps.shape, f32)]
        + [vmem((TABLES + 1, half, half), bf16), vmem((16, channels), f32), rims, rims]
        + [vmem((n * 16, LANES), f32), moved, moved, features, features]
        + [packed, packed, vmem((tokens, LANES), f32), both, both]
        + [spectrum, spectrum] + [products] * 6 + [vmem((2, half, LANES), f32)] * 2
        + [vmem((2, 2, n // 2, rows, LANES), bf16), moved, edges, edges]
        + [quarters, quarters, quarter, quarter, vmem((m, n // m, share, LANES), f32)]
        + [vmem((64, LANES), f32), vmem((64, LANES), bf16), vmem((n, 64, LANES), bf16)]
        + [vmem((tiles, 16, LANES), f32), vmem((tiles, 16, LANES), bf16), vmem((tiles, n, 16, LANES), bf16)]
        + [pltpu.SemaphoreType.DMA((8,)), pltpu.SemaphoreType.DMA((2, 12, n - 1))]
        + [pltpu.SemaphoreType.DMA((2, 2, m - 1))],
        compiler_params=pltpu.CompilerParams(
            collective_id=0, has_side_effects=True, vmem_limit_bytes=56 << 20
        ),
    )(proj_in, out_grad, long_filter, taps, tables_of(tokens, swap_matrix(reps, LANES // reps)))
    out, long_grad, tap_grad = pl.pallas_call(
        hand_over,
        out_shape=tuple(shape(x.shape, x.dtype) for x in (out, long_grad, tap_grad)),
        in_specs=[pl.BlockSpec(memory_space=pl.ANY)] * 3,
        out_specs=[pl.BlockSpec(memory_space=pl.ANY)] * 3,
        scratch_shapes=[pltpu.SemaphoreType.DMA((3,))],
        compiler_params=pltpu.CompilerParams(vmem_limit_bytes=1 << 20),
    )(out, long_grad, tap_grad)
    return (out, long_grad.T, tap_grad)


def fits(n, m, proj_in, taps, long_filter, out_grad):
    streams, rows, channels = proj_in.shape
    groups = long_filter.shape[1]
    if channels % groups or groups % n or n % m or streams != 3 or taps.shape[1] != 3:
        return False
    reps, width = channels // groups, groups // n
    if reps < 2 or reps * width != LANES or n % reps or rows % (8 * reps * m) or rows % LANES:
        return False
    if reps * LANES != n * rows // 2:
        return False
    if n % 8 or n != 2 * reps or reps * 3 + RIM > 16 or 6 * n + RIM > 64 or rows // reps % 16 or n // 2 % reps:
        return False
    return n * rows <= TABLE_LIMIT and n * rows % 1024 == 0


def routed(n, m, *arrays):
    return fast_shards(n, m, *arrays) if fits(n, m, *arrays) else shards(*arrays)


def solution(mesh):
    return jax.shard_map(
        functools.partial(routed, mesh.shape["seq"], mesh.shape["chan"]),
        mesh=mesh,
        in_specs=(P(None, "seq", "chan"), P(None, None, "chan"), P("seq", None), P("seq", "chan")),
        out_specs=(P(None, "seq", "chan"), P("seq", "chan"), P(None, None, "chan")),
        check_vma=False,
    )
```
